32 devices in a mesh: groups: 2 (over x), seq: 16 (over z, y, core).
Axes of the slice: x: 2, y: 2, z: 4, core: 2. Of those that a mesh axis runs over, the one named last changes fastest.
Arguments:
- queries: bfloat16 [1024, 2048], P(('groups', 'seq')), parts along dimension 0, may hold values from -2048 to 2048
- new_keys: bfloat16 [1024, 512], P(('groups', 'seq')), parts along dimension 0, may hold values from -16 to 16
- new_values: bfloat16 [1024, 512], P(('groups', 'seq')), parts along dimension 0, may hold values from -6 to 6
- keys: bfloat16 [131072, 512], P(('groups', 'seq')), parts along dimension 0, may hold values from -16 to 16
- values: bfloat16 [131072, 512], P(('groups', 'seq')), parts along dimension 0, may hold values from -6 to 6
- page_list: int32 [256, 3], P(('groups', 'seq')), parts along dimension 0, may hold values from 0 to 15, as said below
- out_weight: bfloat16 [2048, 4096], P(None, 'seq'), may hold values from -0.125 to 0.125
Outputs:
- projected: bfloat16 [1024, 4096], P(('groups', 'seq')), parts along dimension 0
The draws below stay inside these ranges and needn't reach their ends.
There are 2 independent parts, one for each index of `groups`. The reference program is written for one: setup_inputs(seed, part) draws one part's arguments, and reference() takes and returns one part's arrays. A program takes and returns all parts, laid end to end along the dimension named above; an argument that names none is the same for every part. Nothing has to cross between parts.
Inputs may be any that keep to these rules, and one draw needn't show every extreme that they name: `page_list`: the 3 pages of a tile are distinct. Among the 8 tiles of one index of seq (tiles 8 * i to 8 * (i + 1) - 1) no page is listed more than 3 times, and some page is listed exactly 3 times by the tiles of every index.
All inputs are finite; a program needn't handle non-finite values.
Results may differ from the reference program's by a relative error of at most 0.0058.
Values may be sent and summed in bfloat16 or wider, within the bound.
No kernel may reach another device: no remote copies, remote signals or barrier semaphores. Data moves between devices by JAX's collectives and lax.ppermute only.
A program may use at most 192 MiB of HBM per device.

```python
import math
import jax
import jax.numpy as jnp
from jax import lax

D = 4096
HQ = 16
KVH = 4
HD = 128
PAGE = 4096
QT = 4
TOPK = 3
TILES_DEV = 8
TILES = 128
TOKENS = 512
STORED_BLOCKS = 16
CAP = 3


def page_table(base_key):
    block_directory_seed = jax.random.fold_in(base_key, 11)
    extra_credit_seed, favourite_block_seed, logit_matrix_seed, sequence_rank_seed, shift_amount_seed = jax.random.split(block_directory_seed, 5)
    blocks = TILES // TILES_DEV
    candidates = STORED_BLOCKS * CAP
    ident = jnp.arange(candidates, dtype=jnp.int32)
    owner_page = ident // CAP
    hottest = jax.random.randint(favourite_block_seed, (), 0, STORED_BLOCKS)
    favour_increment = jax.random.randint(extra_credit_seed, (STORED_BLOCKS,), 0, 4) * 1024
    random_part = jax.random.randint(logit_matrix_seed, (blocks, candidates), 0, 1024)
    priority = random_part + favour_increment[owner_page][None, :] + jnp.where(owner_page == hottest, 8192, 0)[None, :]
    priority = priority * candidates + ident[None, :]
    ignored, picked = lax.top_k(priority, TILES_DEV * TOPK)
    picked = jnp.sort(picked, axis=1)
    listed = (picked // CAP).reshape(blocks, TOPK, TILES_DEV).transpose(0, 2, 1)
    orders = jax.vmap(lambda one_key: jax.random.permutation(one_key, TILES_DEV))(jax.random.split(sequence_rank_seed, blocks))
    listed = jnp.take_along_axis(listed, orders[:, :, None], axis=1)
    turned = (jnp.arange(TOPK)[None, None, :] + jax.random.randint(shift_amount_seed, (blocks, TILES_DEV, 1), 0, TOPK)) % TOPK
    listed = jnp.take_along_axis(listed, turned, axis=2)
    return listed.reshape(TILES, TOPK).astype(jnp.int32)


def float_fields(base_key):
    field_key = jax.random.fold_in(base_key, 23)
    subkeys = jax.random.split(field_key, 3)
    rows_all = STORED_BLOCKS * PAGE
    cached = jax.random.truncated_normal(subkeys[0], -6.0, 6.0, (rows_all, KVH * HD), jnp.float32)
    fresh = 1.8 * jax.random.truncated_normal(subkeys[1], -6.0, 6.0, (TILES * QT, KVH * HD), jnp.float32)
    asked = 2.5 * jax.random.truncated_normal(subkeys[2], -6.0, 6.0, (TILES * QT, HQ * HD), jnp.float32)
    return (cached, fresh, asked)


def draw_page_list(key, part):
    return page_table(key)


def draw_keys(key, part):
    return float_fields(key)[0].astype(jnp.bfloat16)


def draw_new_keys(key, part):
    return float_fields(key)[1].astype(jnp.bfloat16)


def draw_queries(key, part):
    return float_fields(key)[2].astype(jnp.bfloat16)


def block_scale(key, shape, shards, low, largest):
    def one(position, parts):
        steps = jax.random.uniform(jax.random.fold_in(jax.random.fold_in(key, 6), position), (parts,), jnp.float32, low / len(shards), largest / len(shards))
        return jnp.repeat(jnp.exp(steps), shape[position] // parts).reshape((-1,) + (1,) * (len(shape) - position - 1))

    gain = one(*shards[0])
    for cut in shards[1:]:
        gain = gain * one(*cut)
    return gain


def scatter_about(key, extent, deviation, limit, cuts=(), kind=jnp.bfloat16):
    factor_of = block_scale(key, extent, cuts, -0.22, 0.18) if cuts else 1.0
    values = jax.random.normal(key, extent, jnp.float32) * deviation * factor_of
    return jnp.minimum(jnp.maximum(values, -limit), limit).astype(kind)


def setup_inputs(seed: int = 0, part: int = 0) -> dict:
    splits = jax.random.split(jax.random.key(seed), 8)
    own_keys = jax.random.split(jax.random.fold_in(splits[7], part), 8)
    return {
        "queries": draw_queries(jax.random.fold_in(jax.random.fold_in(splits[7], part), 71), part),
        "new_keys": draw_new_keys(jax.random.fold_in(jax.random.fold_in(splits[7], part), 71), part),
        "new_values": scatter_about(own_keys[2], (TOKENS, KVH * HD), 1.0, 6.0, ((0, 16),)),
        "keys": draw_keys(jax.random.fold_in(jax.random.fold_in(splits[7], part), 71), part),
        "values": scatter_about(own_keys[4], (STORED_BLOCKS * PAGE, KVH * HD), 1.0, 6.0, ((0, 16),)),
        "page_list": draw_page_list(jax.random.fold_in(jax.random.fold_in(splits[7], part), 71), part),
        "out_weight": scatter_about(splits[6], (HQ * HD, D), (HQ * HD) ** -0.5, 0.125, ((1, 16),)),
    }


def partial_softmax(asked, cached_keys, cached_values, allowed):
    row_count = asked.shape[0]
    per_group = HQ // KVH
    query_full = asked.astype(jnp.float32).reshape(row_count, KVH, per_group, HD)
    key_full = cached_keys.astype(jnp.float32).reshape(-1, KVH, HD)
    value_full = cached_values.astype(jnp.float32).reshape(-1, KVH, HD)
    scores = jnp.einsum('rgjd,lgd->rgjl', query_full, key_full, precision=lax.Precision.HIGHEST) / math.sqrt(HD)
    if allowed is not None:
        scores = jnp.where(allowed[:, None, None, :], scores, -jnp.inf)
    highest = lax.optimization_barrier(jnp.max(scores, axis=-1))
    weights = jnp.exp(scores - highest[..., None])
    summed = lax.optimization_barrier(jnp.sum(weights, axis=-1))
    rounded = lax.optimization_barrier(weights.astype(jnp.bfloat16)).astype(jnp.float32)
    mixed = jnp.einsum('rgjl,lgd->rgjd', rounded, value_full, precision=lax.Precision.HIGHEST) / summed[..., None]
    return (mixed.reshape(row_count, HQ, HD), highest.reshape(row_count, HQ), summed.reshape(row_count, HQ))

def reference(queries, new_keys, new_values, keys, values, page_list, out_weight):

    def one_tile(tile):
        start = (tile * QT).astype(jnp.int32)
        asked = lax.dynamic_slice_in_dim(queries, start, QT, 0)
        fresh_keys = lax.dynamic_slice_in_dim(new_keys, start, QT, 0)
        fresh_values = lax.dynamic_slice_in_dim(new_values, start, QT, 0)
        causal = jnp.arange(QT)[:, None] >= jnp.arange(QT)[None, :]
        own_out, own_max, own_total = partial_softmax(asked, fresh_keys, fresh_values, causal)
        outputs = [own_out]
        maxima = [own_max]
        totals = [own_total]
        for listed in range(TOPK):
            first = (page_list[tile, listed] * PAGE).astype(jnp.int32)
            page_keys = lax.dynamic_slice_in_dim(keys, first, PAGE, 0)
            page_values = lax.dynamic_slice_in_dim(values, first, PAGE, 0)
            page_out, page_max, page_total = partial_softmax(asked, page_keys, page_values, None)
            page_out = lax.optimization_barrier(page_out.astype(jnp.bfloat16)).astype(jnp.float32)
            outputs.append(page_out)
            maxima.append(page_max)
            totals.append(page_total)
        all_max = jnp.stack(maxima)
        all_total = jnp.stack(totals)
        all_out = jnp.stack(outputs)
        top = lax.optimization_barrier(jnp.max(all_max, axis=0))
        factors = all_total * jnp.exp(all_max - top[None])
        numer = lax.optimization_barrier(jnp.sum(factors[..., None] * all_out, axis=0))
        denom = lax.optimization_barrier(jnp.sum(factors, axis=0))
        return (numer / denom[..., None]).reshape(QT, HQ * HD).astype(jnp.bfloat16)
    attended = lax.map(one_tile, jnp.arange(TILES, dtype=jnp.int32)).reshape(TILES * QT, HQ * HD)
    return jnp.dot(attended, out_weight, preferred_element_type=jnp.float32).astype(jnp.bfloat16)
```

```python
import functools
import math

import jax
import jax.numpy as jnp
from jax import lax
from jax.experimental import pallas as pl
from jax.experimental.pallas import tpu as pltpu
from jax.sharding import PartitionSpec as P

HQ = 16
KVH = 4
HD = 128
GROUP = HQ // KVH
LANES = 128
PARTS = 4
STAT_ROWS = KVH * PARTS
SCALE2 = math.log2(math.e) / math.sqrt(HD)
CHUNK = 512


def iota(shape, axis):
    return lax.broadcasted_iota(jnp.int32, shape, axis)


def fill_slots(page_list, base, members, capacity, source, count):
    tiles, width = page_list.shape

    def clear(i, carry):
        source[i] = -1
        return carry

    lax.fori_loop(0, members * capacity, clear, 0)

    def clear_count(i, carry):
        count[i] = 0
        return carry

    lax.fori_loop(0, members, clear_count, 0)
    for tile in range(tiles):
        for item in range(width):
            page = page_list[tile, item] - base

            @pl.when((page >= 0) & (page < members))
            def _():
                slot = count[page]
                source[page * capacity + slot] = tile
                count[page] = slot + 1


def pack_kernel(members, capacity, page_list, queries, packed, source, count):
    tiles = page_list.shape[0]
    rows = queries.shape[0]
    tile_rows = rows // tiles
    slot_rows = capacity * tile_rows
    block = GROUP * slot_rows
    fill_slots(page_list, 0, members, capacity, source, count)
    row = iota((block, GROUP * rows), 0)
    col = iota((block, GROUP * rows), 1)
    fixed = (row // slot_rows == col // rows) & (row % tile_rows == col % tile_rows)
    slot = row % slot_rows // tile_rows
    tile = col % rows // tile_rows
    pieces = []
    for page in range(members):
        wanted = jnp.full((block, GROUP * rows), -1, jnp.int32)
        for k in range(capacity):
            wanted = jnp.where(slot == k, source[page * capacity + k], wanted)
        pieces.append((fixed & (tile == wanted)).astype(jnp.bfloat16))
    chosen = jnp.concatenate(pieces, axis=0)
    for group in range(KVH):
        stacked = jnp.concatenate(
            [
                queries[:, (group * GROUP + j) * HD : (group * GROUP + j + 1) * HD]
                for j in range(GROUP)
            ],
            axis=0,
        )
        sent = jnp.dot(chosen, stacked, preferred_element_type=jnp.float32).astype(jnp.bfloat16)
        packed[:, group * block : (group + 1) * block, :] = sent.reshape(members, block, HD)


def attend_kernel(queries, keys, values, partial, stats):
    members, block, _ = queries.shape
    rows = members * block
    group = pl.program_id(0)
    asked = queries[...].reshape(rows, HD)
    page = keys.shape[0]
    chunk = min(CHUNK, page)
    ones = jnp.ones((chunk, HD), jnp.bfloat16)
    highest = None
    total = None
    for start in range(0, page, chunk):
        scores = lax.dot_general(
            asked,
            keys[start : start + chunk, :],
            (((1,), (1,)), ((), ())),
            preferred_element_type=jnp.float32,
        )
        here = jnp.max(scores, axis=1, keepdims=True)
        new = here if highest is None else jnp.maximum(highest, here)
        weights = jnp.exp2((scores - new) * SCALE2).astype(jnp.bfloat16)
        extended = jnp.concatenate([values[start : start + chunk, :], ones], axis=1)
        mixed = jnp.dot(weights, extended, preferred_element_type=jnp.float32)
        if total is None:
            total = mixed
        else:
            total = total * jnp.exp2((highest - new) * SCALE2) + mixed
        highest = new
    summed = total[:, HD:]
    result = (total[:, :HD] / summed).astype(jnp.bfloat16).reshape(members, block, HD)
    partial[:, pl.ds(pl.multiple_of(group * block, block), block), :] = result
    peak = jnp.broadcast_to(highest * SCALE2, (rows, LANES))
    peak_high = peak.astype(jnp.bfloat16).astype(jnp.float32)
    peak_low = (peak - peak_high).astype(jnp.bfloat16).astype(jnp.float32)
    moved = summed * jnp.exp2(peak - peak_high - peak_low)
    moved_high = moved.astype(jnp.bfloat16).astype(jnp.float32)
    moved_low = moved - moved_high
    part = iota((rows, LANES), 1) % PARTS
    mixed = jnp.where(
        part == 0,
        peak_high,
        jnp.where(part == 1, peak_low, jnp.where(part == 2, moved_high, moved_low)),
    )
    turned = mixed.T[:STAT_ROWS, :]
    mine = iota((STAT_ROWS, rows), 0) // PARTS == group

    @pl.when(group == 0)
    def _():
        stats[...] = turned

    @pl.when(group > 0)
    def _():
        stats[...] = jnp.where(mine, turned, stats[...])

    @pl.when(group == KVH - 1)
    def _():
        padded = jnp.concatenate(
            [stats[...], jnp.zeros((STAT_ROWS, LANES), jnp.float32)], axis=1
        )
        for member in range(members):
            partial[member, KVH * block :, :] = padded[
                :, member * block : member * block + LANES
            ].astype(jnp.bfloat16)


def merge_kernel(
    members, capacity, page_list, queries, new_keys, new_values, returned, attended, source, count
):
    tiles = page_list.shape[0]
    rows = queries.shape[0]
    tile_rows = rows // tiles
    slot_rows = capacity * tile_rows
    block = GROUP * slot_rows
    width = members * block
    tall = GROUP * rows
    fill_slots(page_list, 0, members, capacity, source, count)
    lane = iota((8, width), 1)
    lane_slot = lane // block * capacity + lane % slot_rows // tile_rows
    wanted = jnp.full((8, width), -1, jnp.int32)
    for slot in range(members * capacity):
        wanted = jnp.where(lane_slot == slot, source[slot], wanted)
    lane_code = (wanted * tile_rows + lane % tile_rows) + (lane % block // slot_rows) * rows
    lane_code = jnp.where(wanted < 0, -1, lane_code)[:1, :]
    chosen = iota((tall, width), 0) == lane_code
    bias = jnp.where(chosen, 0.0, -jnp.inf)
    stat_pieces = [
        returned[member, KVH * block :, :].astype(jnp.float32)[:, :block]
        for member in range(members)
    ]
    stats = jnp.concatenate(stat_pieces, axis=1)
    own_row = iota((tall, rows), 0) % rows
    own_col = iota((tall, rows), 1)
    causal = (own_row // tile_rows == own_col // tile_rows) & (own_col <= own_row)
    for group in range(KVH):
        stacked = jnp.concatenate(
            [
                queries[:, (group * GROUP + j) * HD : (group * GROUP + j + 1) * HD]
                for j in range(GROUP)
            ],
            axis=0,
        )
        fresh_keys = new_keys[:, group * HD : (group + 1) * HD]
        fresh_values = new_values[:, group * HD : (group + 1) * HD]
        scores = lax.dot_general(
            stacked, fresh_keys, (((1,), (1,)), ((), ())), preferred_element_type=jnp.float32
        )
        scores = jnp.where(causal, scores, -jnp.inf)
        own_max = jnp.max(scores, axis=1, keepdims=True)
        own_weights = jnp.exp2((scores - own_max) * SCALE2)
        own_total = jnp.sum(own_weights, axis=1, keepdims=True)
        own_sum = jnp.dot(
            own_weights.astype(jnp.bfloat16), fresh_values, preferred_element_type=jnp.float32
        )
        base = group * PARTS
        peak = bias + (stats[base : base + 1, :] + stats[base + 1 : base + 2, :])
        moved = stats[base + 2 : base + 3, :] + stats[base + 3 : base + 4, :]
        own_peak = own_max * SCALE2
        top = jnp.maximum(jnp.max(peak, axis=1, keepdims=True), own_peak)
        factor = jnp.exp2(peak - top) * moved
        own_factor = jnp.exp2(own_peak - top)
        denom = jnp.sum(factor, axis=1, keepdims=True) + own_factor * own_total
        factor = factor / denom
        high = factor.astype(jnp.bfloat16)
        low = (factor - high.astype(jnp.float32)).astype(jnp.bfloat16)
        outs = returned[:, group * block : (group + 1) * block, :].reshape(width, HD)
        numer = (
            jnp.dot(high, outs, preferred_element_type=jnp.float32)
            + jnp.dot(low, outs, preferred_element_type=jnp.float32)
            + own_factor / denom * own_sum
        )
        numer = numer.astype(jnp.bfloat16)
        for j in range(GROUP):
            head = group * GROUP + j
            attended[:, head * HD : (head + 1) * HD] = numer[j * rows : (j + 1) * rows, :]


def project_kernel(count, own, other, place, *refs):
    weights = refs[:count]
    own_out, other_out = refs[count : count + 2]
    held, sems = refs[count + 2 :]
    width = weights[0].shape[1]
    copies = [pltpu.make_async_copy(weights[k], held.at[k], sems.at[k]) for k in range(count)]
    for copy in copies:
        copy.start()
    rows = own.shape[0]
    left = jnp.concatenate([own[...], other[...]], axis=0)
    for k in range(count):
        copies[k].wait()
        made = jnp.dot(left, held[k], preferred_element_type=jnp.float32).astype(jnp.bfloat16)
        at = pl.ds(pl.multiple_of((place[0] ^ k) * width, width), width)
        own_out[:, at] = made[:rows, :]
        other_out[:, at] = made[rows:, :]


VMEM = pl.BlockSpec(memory_space=pltpu.VMEM)
SMEM = pl.BlockSpec(memory_space=pltpu.SMEM)
ANY = pl.BlockSpec(memory_space=pl.ANY)


def slot_scratch(members, capacity):
    return [
        pltpu.SMEM((members * capacity,), jnp.int32),
        pltpu.SMEM((members,), jnp.int32),
    ]


def shards(queries, new_keys, new_values, keys, values, page_list, out_weight):
    members = lax.axis_size("seq")
    me = lax.axis_index("seq")
    tile_count, list_width = page_list.shape
    row_total, features = queries.shape
    tile_rows = row_total // tile_count
    capacity = max(1, 2 * tile_count * list_width // members)
    block = GROUP * capacity * tile_rows
    half = members // 2
    mirror = [(i, (i + half) % members) for i in range(members)]

    packed = pl.pallas_call(
        functools.partial(pack_kernel, members, capacity),
        out_shape=jax.ShapeDtypeStruct((members, KVH * block, HD), jnp.bfloat16),
        in_specs=[SMEM, VMEM],
        out_specs=VMEM,
        scratch_shapes=slot_scratch(members, capacity),
        name="pack",
    )(page_list, queries)
    incoming = lax.all_to_all(packed, "seq", split_axis=0, concat_axis=0, tiled=True)

    page = keys.shape[0]
    rows = members * block
    partial = pl.pallas_call(
        attend_kernel,
        out_shape=jax.ShapeDtypeStruct((members, KVH * block + STAT_ROWS, HD), jnp.bfloat16),
        grid=(KVH,),
        in_specs=[
            pl.BlockSpec((members, block, HD), lambda g: (0, g, 0)),
            pl.BlockSpec((page, HD), lambda g: (0, g)),
            pl.BlockSpec((page, HD), lambda g: (0, g)),
        ],
        out_specs=pl.BlockSpec((members, KVH * block + STAT_ROWS, HD), lambda g: (0, 0, 0)),
        scratch_shapes=[pltpu.VMEM((STAT_ROWS, rows), jnp.float32)],
        compiler_params=pltpu.CompilerParams(
            dimension_semantics=("arbitrary",), vmem_limit_bytes=56 << 20
        ),
        cost_estimate=pl.CostEstimate(
            flops=4 * rows * KVH * page * HD,
            bytes_accessed=4 * page * KVH * HD,
            transcendentals=rows * KVH * page,
        ),
        name="attend",
    )(incoming, keys, values)
    returned = lax.all_to_all(partial, "seq", split_axis=0, concat_axis=0, tiled=True)

    attended = pl.pallas_call(
        functools.partial(merge_kernel, members, capacity),
        out_shape=jax.ShapeDtypeStruct((row_total, features), jnp.bfloat16),
        in_specs=[SMEM] + [VMEM] * 4,
        out_specs=VMEM,
        scratch_shapes=slot_scratch(members, capacity),
        name="merge",
    )(page_list, queries, new_keys, new_values, returned)

    width = out_weight.shape[1]
    if width % LANES or members & (members - 1):
        return jnp.dot(
            attended,
            lax.all_gather(out_weight, "seq", axis=1, tiled=True),
            preferred_element_type=jnp.float32,
        ).astype(jnp.bfloat16)

    def exchanged(array, step):
        return lax.ppermute(array, "seq", [(i, i ^ step) for i in range(members)])

    same_core = [out_weight] + [exchanged(out_weight, step) for step in range(2, half, 2)]
    gathered = []
    for array in same_core:
        gathered += [array, exchanged(array, 1)]
    other = lax.ppermute(attended, "seq", mirror)
    own_out, other_out = pl.pallas_call(
        functools.partial(project_kernel, half),
        out_shape=[jax.ShapeDtypeStruct((row_total, half * width), jnp.bfloat16)] * 2,
        in_specs=[VMEM, VMEM, SMEM] + [ANY] * half,
        out_specs=[VMEM, VMEM],
        scratch_shapes=[
            pltpu.VMEM((half, features, width), jnp.bfloat16),
            pltpu.SemaphoreType.DMA((half,)),
        ],
        name="project",
    )(attended, other, (me % half).reshape(1), *gathered)
    received = lax.ppermute(other_out, "seq", mirror)
    first = me < half
    return jnp.concatenate(
        [jnp.where(first, own_out, received), jnp.where(first, received, own_out)], axis=1
    )


def solution(mesh):
    return jax.shard_map(
        shards,
        mesh=mesh,
        in_specs=(
            P(("groups", "seq"), None),
            P(("groups", "seq"), None),
            P(("groups", "seq"), None),
            P(("groups", "seq"), None),
            P(("groups", "seq"), None),
            P(("groups", "seq"), None),
            P(None, "seq"),
        ),
        out_specs=P(("groups", "seq"), None),
        check_vma=False,
    )
```

```python
import functools
import math

import jax
import jax.numpy as jnp
from jax import lax
from jax.experimental import pallas as pl
from jax.experimental.pallas import tpu as pltpu
from jax.sharding import PartitionSpec as P


HQ = 16
KVH = 4
HD = 128
GROUP = HQ // KVH
LANES = 128
PARTS = 4
STAT_ROWS = KVH * PARTS
SCALE2 = math.log2(math.e) / math.sqrt(HD)
CHUNK = 512
FLOOR = -(2.0**100)


def iota(shape, axis):
    return lax.broadcasted_iota(jnp.int32, shape, axis)


def fill_slots(page_list, base, members, capacity, source, count):
    tiles, width = page_list.shape

    def clear(i, carry):
        source[i] = -1
        return carry

    lax.fori_loop(0, members * capacity, clear, 0)

    def clear_count(i, carry):
        count[i] = 0
        return carry

    lax.fori_loop(0, members, clear_count, 0)
    for tile in range(tiles):
        for item in range(width):
            page = page_list[tile, item] - base

            @pl.when((page >= 0) & (page < members))
            def _():
                slot = count[page]
                source[page * capacity + slot] = tile
                count[page] = slot + 1


def pack_kernel(members, capacity, base, page_list, queries, packed, source, count):
    tiles = page_list.shape[0]
    rows = queries.shape[0]
    tile_rows = rows // tiles
    slot_rows = capacity * tile_rows
    block = GROUP * slot_rows
    fill_slots(page_list, base[0], members, capacity, source, count)
    row = iota((block, GROUP * rows), 0)
    col = iota((block, GROUP * rows), 1)
    fixed = (row // slot_rows == col // rows) & (row % tile_rows == col % tile_rows)
    slot = row % slot_rows // tile_rows
    tile = col % rows // tile_rows
    pieces = []
    for page in range(members):
        wanted = jnp.full((block, GROUP * rows), -1, jnp.int32)
        for k in range(capacity):
            wanted = jnp.where(slot == k, source[page * capacity + k], wanted)
        pieces.append((fixed & (tile == wanted)).astype(jnp.bfloat16))
    chosen = jnp.concatenate(pieces, axis=0)
    for group in range(KVH):
        stacked = jnp.concatenate(
            [
                queries[:, (group * GROUP + j) * HD : (group * GROUP + j + 1) * HD]
                for j in range(GROUP)
            ],
            axis=0,
        )
        sent = jnp.dot(chosen, stacked, preferred_element_type=jnp.float32).astype(jnp.bfloat16)
        packed[:, group * block : (group + 1) * block, :] = sent.reshape(members, block, HD)


def attend_kernel(queries, keys, values, partial, stats):
    members, block, _ = queries.shape
    rows = members * block
    group = pl.program_id(0)
    asked = queries[...].reshape(rows, HD)
    page = keys.shape[0]
    chunk = min(CHUNK, page)
    ones = jnp.ones((chunk, HD), jnp.bfloat16)
    highest = None
    total = None
    for start in range(0, page, chunk):
        scores = lax.dot_general(
            asked,
            keys[start : start + chunk, :],
            (((1,), (1,)), ((), ())),
            preferred_element_type=jnp.float32,
        )
        here = jnp.max(scores, axis=1, keepdims=True)
        new = here if highest is None else jnp.maximum(highest, here)
        weights = jnp.exp2((scores - new) * SCALE2).astype(jnp.bfloat16)
        extended = jnp.concatenate([values[start : start + chunk, :], ones], axis=1)
        mixed = jnp.dot(weights, extended, preferred_element_type=jnp.float32)
        if total is None:
            total = mixed
        else:
            total = total * jnp.exp2((highest - new) * SCALE2) + mixed
        highest = new
    summed = total[:, HD:]
    result = (total[:, :HD] / summed).astype(jnp.bfloat16).reshape(members, block, HD)
    partial[:, pl.ds(pl.multiple_of(group * block, block), block), :] = result
    peak = jnp.broadcast_to(highest * SCALE2, (rows, LANES))
    peak_high = peak.astype(jnp.bfloat16).astype(jnp.float32)
    peak_low = (peak - peak_high).astype(jnp.bfloat16).astype(jnp.float32)
    moved = summed * jnp.exp2(peak - peak_high - peak_low)
    moved_high = moved.astype(jnp.bfloat16).astype(jnp.float32)
    moved_low = moved - moved_high
    part = iota((rows, LANES), 1) % PARTS
    mixed = jnp.where(
        part == 0,
        peak_high,
        jnp.where(part == 1, peak_low, jnp.where(part == 2, moved_high, moved_low)),
    )
    turned = mixed.T[:STAT_ROWS, :]
    mine = iota((STAT_ROWS, rows), 0) // PARTS == group

    @pl.when(group == 0)
    def _():
        stats[...] = turned

    @pl.when(group > 0)
    def _():
        stats[...] = jnp.where(mine, turned, stats[...])

    @pl.when(group == KVH - 1)
    def _():
        padded = jnp.concatenate(
            [stats[...], jnp.zeros((STAT_ROWS, LANES), jnp.float32)], axis=1
        )
        for member in range(members):
            partial[member, KVH * block :, :] = padded[
                :, member * block : member * block + LANES
            ].astype(jnp.bfloat16)


def split(value):
    high = value.astype(jnp.bfloat16).astype(jnp.float32)
    return high, (value - high).astype(jnp.bfloat16).astype(jnp.float32)


def stacked_heads(queries, group):
    return jnp.concatenate(
        [
            queries[:, (group * GROUP + j) * HD : (group * GROUP + j + 1) * HD]
            for j in range(GROUP)
        ],
        axis=0,
    )


def own_partial(queries, new_keys, new_values, causal, group):
    scores = lax.dot_general(
        stacked_heads(queries, group),
        new_keys[:, group * HD : (group + 1) * HD],
        (((1,), (1,)), ((), ())),
        preferred_element_type=jnp.float32,
    )
    scores = jnp.where(causal, scores, -jnp.inf)
    peak = jnp.max(scores, axis=1, keepdims=True)
    weights = jnp.exp2((scores - peak) * SCALE2)
    total = jnp.sum(weights, axis=1, keepdims=True)
    mixed = jnp.dot(
        weights.astype(jnp.bfloat16),
        new_values[:, group * HD : (group + 1) * HD],
        preferred_element_type=jnp.float32,
    )
    return peak * SCALE2, total, mixed


def merge_kernel(members, capacity, with_own, base, page_list, *refs):
    own_refs = refs[:3] if with_own else ()
    returned, merged, source, count = refs[len(own_refs) :]
    tiles = page_list.shape[0]
    tall = (merged.shape[0] - STAT_ROWS) // KVH
    rows = tall // GROUP
    tile_rows = rows // tiles
    slot_rows = capacity * tile_rows
    block = GROUP * slot_rows
    width = members * block
    fill_slots(page_list, base[0], members, capacity, source, count)
    lane = iota((8, width), 1)
    lane_slot = lane // block * capacity + lane % slot_rows // tile_rows
    wanted = jnp.full((8, width), -1, jnp.int32)
    for slot in range(members * capacity):
        wanted = jnp.where(lane_slot == slot, source[slot], wanted)
    lane_code = (wanted * tile_rows + lane % tile_rows) + (lane % block // slot_rows) * rows
    lane_code = jnp.where(wanted < 0, -1, lane_code)[:1, :]
    bias = jnp.where(iota((tall, width), 0) == lane_code, 0.0, -jnp.inf)
    stat_pieces = [
        returned[member, KVH * block :, :].astype(jnp.float32)[:, :block]
        for member in range(members)
    ]
    stats = jnp.concatenate(stat_pieces, axis=1)
    if with_own:
        own_row = iota((tall, rows), 0) % rows
        own_col = iota((tall, rows), 1)
        causal = (own_row // tile_rows == own_col // tile_rows) & (own_col <= own_row)
    part = iota((tall, LANES), 1)
    columns = jnp.zeros((tall, LANES), jnp.float32)
    for group in range(KVH):
        at = group * PARTS
        peak = bias + (stats[at : at + 1, :] + stats[at + 1 : at + 2, :])
        moved = stats[at + 2 : at + 3, :] + stats[at + 3 : at + 4, :]
        top = jnp.maximum(jnp.max(peak, axis=1, keepdims=True), FLOOR)
        if with_own:
            own_peak, own_total, own_sum = own_partial(*own_refs, causal, group)
            top = jnp.maximum(top, own_peak)
        factor = jnp.exp2(peak - top) * moved
        denom = jnp.sum(factor, axis=1, keepdims=True)
        if with_own:
            own_factor = jnp.exp2(own_peak - top)
            denom = denom + own_factor * own_total
        inverse = 1.0 / jnp.where(denom > 0.0, denom, 1.0)
        factor = factor * inverse
        high = factor.astype(jnp.bfloat16)
        low = (factor - high.astype(jnp.float32)).astype(jnp.bfloat16)
        outs = returned[:, group * block : (group + 1) * block, :].reshape(width, HD)
        numer = jnp.dot(high, outs, preferred_element_type=jnp.float32) + jnp.dot(
            low, outs, preferred_element_type=jnp.float32
        )
        if with_own:
            numer = numer + own_factor * inverse * own_sum
        merged[group * tall : (group + 1) * tall, :] = numer.astype(jnp.bfloat16)
        peak_high, peak_low = split(top)
        moved_high, moved_low = split(denom * jnp.exp2(top - peak_high - peak_low))
        for i, value in enumerate((peak_high, peak_low, moved_high, moved_low)):
            columns = jnp.where(part == at + i, value, columns)
    merged[KVH * tall :, :tall] = columns.T[:STAT_ROWS, :].astype(jnp.bfloat16)


def combine(tall, first, second):
    rows = tall // GROUP
    a = first[KVH * tall :, :].astype(jnp.float32)
    b = second[KVH * tall :, :].astype(jnp.float32)
    shares = []
    for group in range(KVH):
        at = group * PARTS
        a_peak = a[at : at + 1, :] + a[at + 1 : at + 2, :]
        b_peak = b[at : at + 1, :] + b[at + 1 : at + 2, :]
        a_total = a[at + 2 : at + 3, :] + a[at + 3 : at + 4, :]
        b_total = b[at + 2 : at + 3, :] + b[at + 3 : at + 4, :]
        top = jnp.maximum(a_peak, b_peak)
        a_factor = a_total * jnp.exp2(a_peak - top)
        b_factor = b_total * jnp.exp2(b_peak - top)
        denom = a_factor + b_factor
        shares += [a_factor / denom, b_factor / denom]
    shares = jnp.concatenate(
        shares + [jnp.zeros((LANES - len(shares), LANES), jnp.float32)], axis=0
    ).T
    heads = []
    for group in range(KVH):
        rows_at = slice(group * tall, (group + 1) * tall)
        mixed = (
            first[rows_at, :].astype(jnp.float32) * shares[:tall, 2 * group : 2 * group + 1]
            + second[rows_at, :].astype(jnp.float32)
            * shares[:tall, 2 * group + 1 : 2 * group + 2]
        ).astype(jnp.bfloat16)
        heads += [mixed[j * rows : (j + 1) * rows, :] for j in range(GROUP)]
    return jnp.concatenate(heads, axis=1)


def attended_kernel(first, second, attended):
    tall = (first.shape[0] - STAT_ROWS) // KVH
    attended[...] = combine(tall, first, second)


def project_kernel(count, places, own_a, own_b, other_a, other_b, me, *refs):
    weights = refs[: len(places)]
    own_out, other_out = refs[len(places) : len(places) + 2]
    held, sems = refs[len(places) + 2 :]
    width = weights[0].shape[1]
    copies = {k: [] for k in range(count)}
    for i, (k, start) in enumerate(places):
        copy = pltpu.make_async_copy(
            weights[i], held.at[k, start : start + weights[i].shape[0], :], sems.at[i]
        )
        copy.start()
        copies[k].append(copy)
    tall = (own_a.shape[0] - STAT_ROWS) // KVH
    rows = tall // GROUP
    left = jnp.concatenate(
        [combine(tall, own_a, own_b), combine(tall, other_a, other_b)], axis=0
    )
    for k in range(count):
        for copy in copies[k]:
            copy.wait()
        made = jnp.dot(left, held[k], preferred_element_type=jnp.float32).astype(jnp.bfloat16)
        at = pl.ds(pl.multiple_of((me[0] ^ k) * width, width), width)
        own_out[:, at] = made[:rows, :]
        other_out[:, at] = made[rows:, :]


VMEM = pl.BlockSpec(memory_space=pltpu.VMEM)
SMEM = pl.BlockSpec(memory_space=pltpu.SMEM)
ANY = pl.BlockSpec(memory_space=pl.ANY)
SMALL = pltpu.CompilerParams(vmem_limit_bytes=16 << 20)


def slot_scratch(members, capacity):
    return [
        pltpu.SMEM((members * capacity,), jnp.int32),
        pltpu.SMEM((members,), jnp.int32),
    ]


def shards(queries, new_keys, new_values, keys, values, page_list, out_weight):
    members = lax.axis_size("seq")
    me = lax.axis_index("seq")
    tile_count, list_width = page_list.shape
    row_total, features = queries.shape
    tile_rows = row_total // tile_count
    capacity = max(1, 2 * tile_count * list_width // members)
    block = GROUP * capacity * tile_rows
    half = members // 2
    tall = GROUP * row_total
    halves = [list(range(half)), list(range(half, members))]
    base = (me // half * half).reshape(1)
    page = keys.shape[0]
    rows = half * block

    def mirrored(array):
        return lax.ppermute(array, "seq", [(i, (i + half) % members) for i in range(members)])

    def pack(tiles, listed):
        return pl.pallas_call(
            functools.partial(pack_kernel, half, capacity),
            out_shape=jax.ShapeDtypeStruct((half, KVH * block, HD), jnp.bfloat16),
            in_specs=[SMEM, SMEM, VMEM],
            out_specs=VMEM,
            scratch_shapes=slot_scratch(half, capacity),
            compiler_params=SMALL,
            name="pack",
        )(base, listed, tiles)

    def spread(array):
        return lax.all_to_all(
            array, "seq", split_axis=0, concat_axis=0, tiled=True, axis_index_groups=halves
        )

    def attend(incoming):
        return pl.pallas_call(
            attend_kernel,
            out_shape=jax.ShapeDtypeStruct((half, KVH * block + STAT_ROWS, HD), jnp.bfloat16),
            grid=(KVH,),
            in_specs=[
                pl.BlockSpec((half, block, HD), lambda g: (0, g, 0)),
                pl.BlockSpec((page, HD), lambda g: (0, g)),
                pl.BlockSpec((page, HD), lambda g: (0, g)),
            ],
            out_specs=pl.BlockSpec((half, KVH * block + STAT_ROWS, HD), lambda g: (0, 0, 0)),
            scratch_shapes=[pltpu.VMEM((STAT_ROWS, rows), jnp.float32)],
            compiler_params=pltpu.CompilerParams(
                dimension_semantics=("arbitrary",), vmem_limit_bytes=58 << 20
            ),
            cost_estimate=pl.CostEstimate(
                flops=4 * rows * KVH * page * HD,
                bytes_accessed=4 * page * KVH * HD,
                transcendentals=rows * KVH * page,
            ),
            name="attend",
        )(incoming, keys, values)

    def merge(listed, returned, own):
        return pl.pallas_call(
            functools.partial(merge_kernel, half, capacity, bool(own)),
            out_shape=jax.ShapeDtypeStruct((KVH * tall + STAT_ROWS, HD), jnp.bfloat16),
            in_specs=[SMEM, SMEM] + [VMEM] * (len(own) + 1),
            out_specs=VMEM,
            scratch_shapes=slot_scratch(half, capacity),
            compiler_params=SMALL,
            name="merge",
        )(base, listed, *own, returned)

    other_queries = mirrored(queries)
    other_list = mirrored(page_list)
    packed_near = pack(queries, page_list)
    near = spread(packed_near)
    packed_far = pack(other_queries, other_list)
    far = spread(packed_far)
    near_partial = attend(near)
    near_back = spread(near_partial)
    far_partial = attend(far)
    far_back = spread(far_partial)
    own_a = merge(page_list, near_back, (queries, new_keys, new_values))
    other_b = merge(other_list, far_back, ())
    other_a = mirrored(own_a)
    own_b = mirrored(other_b)

    width = out_weight.shape[1]
    if width % LANES or members & (members - 1):
        attended = pl.pallas_call(
            attended_kernel,
            out_shape=jax.ShapeDtypeStruct((row_total, features), jnp.bfloat16),
            in_specs=[VMEM, VMEM],
            out_specs=VMEM,
            name="combine",
        )(own_a, own_b)
        return jnp.dot(
            attended,
            lax.all_gather(out_weight, "seq", axis=1, tiled=True),
            preferred_element_type=jnp.float32,
        ).astype(jnp.bfloat16)

    def exchanged(array, step):
        return lax.ppermute(array, "seq", [(i, i ^ step) for i in range(members)])

    middle = features // 2

    def upper(pieces):
        return pieces[0] if len(pieces) > 1 else pieces[0][:middle, :]

    def lower(pieces):
        return pieces[1] if len(pieces) > 1 else pieces[0][middle:, :]

    same_core = {0: [out_weight]}
    for step in range(2, half, 2):
        low = step & -step
        if low == step:
            same_core[step] = [exchanged(out_weight, step)]
    for step in range(2, half, 2):
        low = step & -step
        if low != step:
            same_core[step] = [
                exchanged(upper(same_core[step ^ low]), low),
                exchanged(lower(same_core[low]), step ^ low),
            ]
    gathered = []
    places = []
    for step, pieces in same_core.items():
        for i, piece in enumerate(pieces):
            gathered += [piece, exchanged(piece, 1)]
            places += [(step, i * middle), (step + 1, i * middle)]
    own_out, other_out = pl.pallas_call(
        functools.partial(project_kernel, half, tuple(places)),
        out_shape=[jax.ShapeDtypeStruct((row_total, half * width), jnp.bfloat16)] * 2,
        in_specs=[VMEM] * 4 + [SMEM] + [ANY] * len(places),
        out_specs=[VMEM, VMEM],
        scratch_shapes=[
            pltpu.VMEM((half, features, width), jnp.bfloat16),
            pltpu.SemaphoreType.DMA((len(places),)),
        ],
        compiler_params=pltpu.CompilerParams(vmem_limit_bytes=60 << 20),
        name="project",
    )(own_a, own_b, other_a, other_b, (me % half).reshape(1), *gathered)
    received = mirrored(other_out)
    first = me < half
    return jnp.concatenate(
        [jnp.where(first, own_out, received), jnp.where(first, received, own_out)], axis=1
    )


def solution(mesh):
    return jax.shard_map(
        shards,
        mesh=mesh,
        in_specs=(
            P(("groups", "seq"), None),
            P(("groups", "seq"), None),
            P(("groups", "seq"), None),
            P(("groups", "seq"), None),
            P(("groups", "seq"), None),
            P(("groups", "seq"), None),
            P(None, "seq"),
        ),
        out_specs=P(("groups", "seq"), None),
        check_vma=False,
    )
```

```python
import functools
import math

import jax
import jax.numpy as jnp
from jax import lax
from jax.experimental import pallas as pl
from jax.experimental.pallas import tpu as pltpu
from jax.sharding import PartitionSpec as P


HQ = 16
KVH = 4
HD = 128
GROUP = HQ // KVH
LANES = 128
PARTS = 4
STAT_ROWS = KVH * PARTS
SCALE2 = math.log2(math.e) / math.sqrt(HD)
CHUNK = 512
AHEAD = 3
FLOOR = -(2.0**100)


def iota(shape, axis):
    return lax.broadcasted_iota(jnp.int32, shape, axis)


def fill_slots(page_list, base, members, capacity, source, count):
    tiles, width = page_list.shape

    def clear(i, carry):
        source[i] = -1
        return carry

    lax.fori_loop(0, members * capacity, clear, 0)

    def clear_count(i, carry):
        count[i] = 0
        return carry

    lax.fori_loop(0, members, clear_count, 0)
    for tile in range(tiles):
        for item in range(width):
            page = page_list[tile, item] - base

            @pl.when((page >= 0) & (page < members))
            def _():
                slot = count[page]
                source[page * capacity + slot] = tile
                count[page] = slot + 1


def pack_kernel(members, capacity, base, page_list, queries, packed, source, count):
    tiles = page_list.shape[0]
    rows = queries.shape[0]
    tile_rows = rows // tiles
    slot_rows = capacity * tile_rows
    block = GROUP * slot_rows
    fill_slots(page_list, base[0], members, capacity, source, count)
    row = iota((block, GROUP * rows), 0)
    col = iota((block, GROUP * rows), 1)
    fixed = (row // slot_rows == col // rows) & (row % tile_rows == col % tile_rows)
    slot = row % slot_rows // tile_rows
    tile = col % rows // tile_rows
    pieces = []
    for page in range(members):
        wanted = jnp.full((block, GROUP * rows), -1, jnp.int32)
        for k in range(capacity):
            wanted = jnp.where(slot == k, source[page * capacity + k], wanted)
        pieces.append((fixed & (tile == wanted)).astype(jnp.bfloat16))
    chosen = jnp.concatenate(pieces, axis=0)
    for group in range(KVH):
        stacked = jnp.concatenate(
            [
                queries[:, (group * GROUP + j) * HD : (group * GROUP + j + 1) * HD]
                for j in range(GROUP)
            ],
            axis=0,
        )
        sent = jnp.dot(chosen, stacked, preferred_element_type=jnp.float32).astype(jnp.bfloat16)
        packed[:, group * block : (group + 1) * block, :] = sent.reshape(members, block, HD)


def attend_kernel(queries, keys, values, partial, stats):
    members, block, _ = queries.shape
    rows = members * block
    group = pl.program_id(0)
    asked = queries[...].reshape(rows, HD)
    page = keys.shape[0]
    chunk = min(CHUNK, page)
    ones = jnp.ones((chunk, HD), jnp.bfloat16)
    highest = None
    total = None
    for start in range(0, page, chunk):
        scores = lax.dot_general(
            asked,
            keys[start : start + chunk, :],
            (((1,), (1,)), ((), ())),
            preferred_element_type=jnp.float32,
        )
        here = jnp.max(scores, axis=1, keepdims=True)
        new = here if highest is None else jnp.maximum(highest, here)
        weights = jnp.exp2((scores - new) * SCALE2).astype(jnp.bfloat16)
        extended = jnp.concatenate([values[start : start + chunk, :], ones], axis=1)
        mixed = jnp.dot(weights, extended, preferred_element_type=jnp.float32)
        if total is None:
            total = mixed
        else:
            total = total * jnp.exp2((highest - new) * SCALE2) + mixed
        highest = new
    summed = total[:, HD:]
    result = (total[:, :HD] / summed).astype(jnp.bfloat16).reshape(members, block, HD)
    partial[:, pl.ds(pl.multiple_of(group * block, block), block), :] = result
    peak = jnp.broadcast_to(highest * SCALE2, (rows, LANES))
    peak_high = peak.astype(jnp.bfloat16).astype(jnp.float32)
    peak_low = (peak - peak_high).astype(jnp.bfloat16).astype(jnp.float32)
    moved = summed * jnp.exp2(peak - peak_high - peak_low)
    moved_high = moved.astype(jnp.bfloat16).astype(jnp.float32)
    moved_low = moved - moved_high
    part = iota((rows, LANES), 1) % PARTS
    mixed = jnp.where(
        part == 0,
        peak_high,
        jnp.where(part == 1, peak_low, jnp.where(part == 2, moved_high, moved_low)),
    )
    turned = mixed.T[:STAT_ROWS, :]
    mine = iota((STAT_ROWS, rows), 0) // PARTS == group

    @pl.when(group == 0)
    def _():
        stats[...] = turned

    @pl.when(group > 0)
    def _():
        stats[...] = jnp.where(mine, turned, stats[...])

    @pl.when(group == KVH - 1)
    def _():
        padded = jnp.concatenate(
            [stats[...], jnp.zeros((STAT_ROWS, LANES), jnp.float32)], axis=1
        )
        for member in range(members):
            partial[member, KVH * block :, :] = padded[
                :, member * block : member * block + LANES
            ].astype(jnp.bfloat16)


def split(value):
    high = value.astype(jnp.bfloat16).astype(jnp.float32)
    return high, (value - high).astype(jnp.bfloat16).astype(jnp.float32)


def stacked_heads(queries, group):
    return jnp.concatenate(
        [
            queries[:, (group * GROUP + j) * HD : (group * GROUP + j + 1) * HD]
            for j in range(GROUP)
        ],
        axis=0,
    )


def own_partial(queries, new_keys, new_values, causal, group):
    scores = lax.dot_general(
        stacked_heads(queries, group),
        new_keys[:, group * HD : (group + 1) * HD],
        (((1,), (1,)), ((), ())),
        preferred_element_type=jnp.float32,
    )
    scores = jnp.where(causal, scores, -jnp.inf)
    peak = jnp.max(scores, axis=1, keepdims=True)
    weights = jnp.exp2((scores - peak) * SCALE2)
    total = jnp.sum(weights, axis=1, keepdims=True)
    mixed = jnp.dot(
        weights.astype(jnp.bfloat16),
        new_values[:, group * HD : (group + 1) * HD],
        preferred_element_type=jnp.float32,
    )
    return peak * SCALE2, total, mixed


def merge_kernel(members, capacity, with_own, base, page_list, *refs):
    own_refs = refs[:3] if with_own else ()
    returned, merged, source, count = refs[len(own_refs) :]
    tiles = page_list.shape[0]
    tall = (merged.shape[0] - STAT_ROWS) // KVH
    rows = tall // GROUP
    tile_rows = rows // tiles
    slot_rows = capacity * tile_rows
    block = GROUP * slot_rows
    width = members * block
    fill_slots(page_list, base[0], members, capacity, source, count)
    lane = iota((8, width), 1)
    lane_slot = lane // block * capacity + lane % slot_rows // tile_rows
    wanted = jnp.full((8, width), -1, jnp.int32)
    for slot in range(members * capacity):
        wanted = jnp.where(lane_slot == slot, source[slot], wanted)
    lane_code = (wanted * tile_rows + lane % tile_rows) + (lane % block // slot_rows) * rows
    lane_code = jnp.where(wanted < 0, -1, lane_code)[:1, :]
    bias = jnp.where(iota((tall, width), 0) == lane_code, 0.0, -jnp.inf)
    stat_pieces = [
        returned[member, KVH * block :, :].astype(jnp.float32)[:, :block]
        for member in range(members)
    ]
    stats = jnp.concatenate(stat_pieces, axis=1)
    if with_own:
        own_row = iota((tall, rows), 0) % rows
        own_col = iota((tall, rows), 1)
        causal = (own_row // tile_rows == own_col // tile_rows) & (own_col <= own_row)
    part = iota((tall, LANES), 1)
    columns = jnp.zeros((tall, LANES), jnp.float32)
    for group in range(KVH):
        at = group * PARTS
        peak = bias + (stats[at : at + 1, :] + stats[at + 1 : at + 2, :])
        moved = stats[at + 2 : at + 3, :] + stats[at + 3 : at + 4, :]
        top = jnp.maximum(jnp.max(peak, axis=1, keepdims=True), FLOOR)
        if with_own:
            own_peak, own_total, own_sum = own_partial(*own_refs, causal, group)
            top = jnp.maximum(top, own_peak)
        factor = jnp.exp2(peak - top) * moved
        denom = jnp.sum(factor, axis=1, keepdims=True)
        if with_own:
            own_factor = jnp.exp2(own_peak - top)
            denom = denom + own_factor * own_total
        inverse = 1.0 / jnp.where(denom > 0.0, denom, 1.0)
        factor = factor * inverse
        high = factor.astype(jnp.bfloat16)
        low = (factor - high.astype(jnp.float32)).astype(jnp.bfloat16)
        outs = returned[:, group * block : (group + 1) * block, :].reshape(width, HD)
        numer = jnp.dot(high, outs, preferred_element_type=jnp.float32) + jnp.dot(
            low, outs, preferred_element_type=jnp.float32
        )
        if with_own:
            numer = numer + own_factor * inverse * own_sum
        merged[group * tall : (group + 1) * tall, :] = numer.astype(jnp.bfloat16)
        peak_high, peak_low = split(top)
        moved_high, moved_low = split(denom * jnp.exp2(top - peak_high - peak_low))
        for i, value in enumerate((peak_high, peak_low, moved_high, moved_low)):
            columns = jnp.where(part == at + i, value, columns)
    merged[KVH * tall :, :tall] = columns.T[:STAT_ROWS, :].astype(jnp.bfloat16)


def combine(tall, first, second):
    rows = tall // GROUP
    a = first[KVH * tall :, :].astype(jnp.float32)
    b = second[KVH * tall :, :].astype(jnp.float32)
    shares = []
    for group in range(KVH):
        at = group * PARTS
        a_peak = a[at : at + 1, :] + a[at + 1 : at + 2, :]
        b_peak = b[at : at + 1, :] + b[at + 1 : at + 2, :]
        a_total = a[at + 2 : at + 3, :] + a[at + 3 : at + 4, :]
        b_total = b[at + 2 : at + 3, :] + b[at + 3 : at + 4, :]
        top = jnp.maximum(a_peak, b_peak)
        a_factor = a_total * jnp.exp2(a_peak - top)
        b_factor = b_total * jnp.exp2(b_peak - top)
        denom = a_factor + b_factor
        shares += [a_factor / denom, b_factor / denom]
    shares = jnp.concatenate(
        shares + [jnp.zeros((LANES - len(shares), LANES), jnp.float32)], axis=0
    ).T
    heads = []
    for group in range(KVH):
        rows_at = slice(group * tall, (group + 1) * tall)
        mixed = (
            first[rows_at, :].astype(jnp.float32) * shares[:tall, 2 * group : 2 * group + 1]
            + second[rows_at, :].astype(jnp.float32)
            * shares[:tall, 2 * group + 1 : 2 * group + 2]
        ).astype(jnp.bfloat16)
        heads += [mixed[j * rows : (j + 1) * rows, :] for j in range(GROUP)]
    return jnp.concatenate(heads, axis=1)


def attended_kernel(first, second, attended):
    tall = (first.shape[0] - STAT_ROWS) // KVH
    attended[...] = combine(tall, first, second)


def project_kernel(count, places, own_a, own_b, other_a, other_b, me, *refs):
    weights = refs[: len(places)]
    own_out, other_out = refs[len(places) : len(places) + 2]
    held, sems = refs[len(places) + 2 :]
    width = weights[0].shape[1]
    copies = {k: [] for k in range(count)}
    for i, (k, start) in enumerate(places):
        copies[k].append(
            pltpu.make_async_copy(
                weights[i], held.at[k, start : start + weights[i].shape[0], :], sems.at[i]
            )
        )
    order = [copies[k] for k in range(count)]
    ahead = min(AHEAD, count)
    for group in order[:ahead]:
        for copy in group:
            copy.start()
    tall = (own_a.shape[0] - STAT_ROWS) // KVH
    rows = tall // GROUP
    left = jnp.concatenate(
        [combine(tall, own_a, own_b), combine(tall, other_a, other_b)], axis=0
    )
    for k in range(count):
        for copy in copies[k]:
            copy.wait()
        if k + ahead < count:
            for copy in order[k + ahead]:
                copy.start()
        made = jnp.dot(left, held[k], preferred_element_type=jnp.float32).astype(jnp.bfloat16)
        at = pl.ds(pl.multiple_of((me[0] ^ k) * width, width), width)
        own_out[:, at] = made[:rows, :]
        other_out[:, at] = made[rows:, :]


def place_kernel(first, own, received, out):
    width = own.shape[1]
    out[:, pl.ds(pl.multiple_of(first[0] * width, width), width)] = own[...]
    out[:, pl.ds(pl.multiple_of((1 - first[0]) * width, width), width)] = received[...]


VMEM = pl.BlockSpec(memory_space=pltpu.VMEM)
SMEM = pl.BlockSpec(memory_space=pltpu.SMEM)
ANY = pl.BlockSpec(memory_space=pl.ANY)
LARGE = pltpu.CompilerParams(vmem_limit_bytes=60 << 20)
SMALL = pltpu.CompilerParams(vmem_limit_bytes=16 << 20)


def slot_scratch(members, capacity):
    return [
        pltpu.SMEM((members * capacity,), jnp.int32),
        pltpu.SMEM((members,), jnp.int32),
    ]


def early_first(step):
    return (1, 0) if step == 2 else (0, 1)


def shards(queries, new_keys, new_values, keys, values, page_list, out_weight):
    members = lax.axis_size("seq")
    me = lax.axis_index("seq")
    tile_count, list_width = page_list.shape
    row_total, features = queries.shape
    tile_rows = row_total // tile_count
    capacity = max(1, 2 * tile_count * list_width // members)
    block = GROUP * capacity * tile_rows
    half = members // 2
    tall = GROUP * row_total
    halves = [list(range(half)), list(range(half, members))]
    base = (me // half * half).reshape(1)
    page = keys.shape[0]
    rows = half * block

    def mirrored(array):
        return lax.ppermute(array, "seq", [(i, (i + half) % members) for i in range(members)])

    def pack(tiles, listed, params):
        return pl.pallas_call(
            functools.partial(pack_kernel, half, capacity),
            out_shape=jax.ShapeDtypeStruct((half, KVH * block, HD), jnp.bfloat16),
            in_specs=[SMEM, SMEM, VMEM],
            out_specs=VMEM,
            scratch_shapes=slot_scratch(half, capacity),
            compiler_params=params,
            name="pack",
        )(base, listed, tiles)

    def spread(array):
        return lax.all_to_all(
            array, "seq", split_axis=0, concat_axis=0, tiled=True, axis_index_groups=halves
        )

    def attend(incoming):
        return pl.pallas_call(
            attend_kernel,
            out_shape=jax.ShapeDtypeStruct((half, KVH * block + STAT_ROWS, HD), jnp.bfloat16),
            grid=(KVH,),
            in_specs=[
                pl.BlockSpec((half, block, HD), lambda g: (0, g, 0)),
                pl.BlockSpec((page, HD), lambda g: (0, g)),
                pl.BlockSpec((page, HD), lambda g: (0, g)),
            ],
            out_specs=pl.BlockSpec((half, KVH * block + STAT_ROWS, HD), lambda g: (0, 0, 0)),
            scratch_shapes=[pltpu.VMEM((STAT_ROWS, rows), jnp.float32)],
            compiler_params=pltpu.CompilerParams(
                dimension_semantics=("arbitrary",), vmem_limit_bytes=58 << 20
            ),
            cost_estimate=pl.CostEstimate(
                flops=4 * rows * KVH * page * HD,
                bytes_accessed=4 * page * KVH * HD,
                transcendentals=rows * KVH * page,
            ),
            name="attend",
        )(incoming, keys, values)

    def merge(listed, returned, own):
        return pl.pallas_call(
            functools.partial(merge_kernel, half, capacity, bool(own)),
            out_shape=jax.ShapeDtypeStruct((KVH * tall + STAT_ROWS, HD), jnp.bfloat16),
            in_specs=[SMEM, SMEM] + [VMEM] * (len(own) + 1),
            out_specs=VMEM,
            scratch_shapes=slot_scratch(half, capacity),
            compiler_params=SMALL,
            name="merge",
        )(base, listed, *own, returned)

    other_queries = mirrored(queries)
    other_list = mirrored(page_list)
    packed_near = pack(queries, page_list, LARGE)
    near = spread(packed_near)
    packed_far = pack(other_queries, other_list, SMALL)
    far = spread(packed_far)
    near_partial = attend(near)
    near_back = spread(near_partial)
    far_partial = attend(far)
    far_back = spread(far_partial)
    own_a = merge(page_list, near_back, (queries, new_keys, new_values))
    other_b = merge(other_list, far_back, ())
    other_a = mirrored(own_a)
    own_b = mirrored(other_b)

    width = out_weight.shape[1]
    if width % LANES or members & (members - 1):
        attended = pl.pallas_call(
            attended_kernel,
            out_shape=jax.ShapeDtypeStruct((row_total, features), jnp.bfloat16),
            in_specs=[VMEM, VMEM],
            out_specs=VMEM,
            name="combine",
        )(own_a, own_b)
        return jnp.dot(
            attended,
            lax.all_gather(out_weight, "seq", axis=1, tiled=True),
            preferred_element_type=jnp.float32,
        ).astype(jnp.bfloat16)

    def exchanged(array, step):
        return lax.ppermute(array, "seq", [(i, i ^ step) for i in range(members)])

    middle = features // 2
    halves_of = [out_weight[:middle, :], out_weight[middle:, :]]
    pieces = {0: [out_weight]}
    for step in range(2, half, 2):
        low = step & -step
        if low == step:
            pieces[step] = [None, None]
            for i in early_first(step):
                pieces[step][i] = exchanged(halves_of[i], step)
    for step in range(2, half, 2):
        low = step & -step
        if low != step:
            first_piece = exchanged(pieces[step ^ low][0], low)
            pieces[step] = [first_piece, exchanged(pieces[low][1], step ^ low)]
    gathered = []
    places = []
    for step, parts in pieces.items():
        for i, part in enumerate(parts):
            gathered += [part, exchanged(part, 1)]
            places += [(step, i * middle), (step + 1, i * middle)]
    own_out, other_out = pl.pallas_call(
        functools.partial(project_kernel, half, tuple(places)),
        out_shape=[jax.ShapeDtypeStruct((row_total, half * width), jnp.bfloat16)] * 2,
        in_specs=[VMEM] * 4 + [SMEM] + [ANY] * len(places),
        out_specs=[VMEM, VMEM],
        scratch_shapes=[
            pltpu.VMEM((half, features, width), jnp.bfloat16),
            pltpu.SemaphoreType.DMA((len(places),)),
        ],
        compiler_params=LARGE,
        name="project",
    )(own_a, own_b, other_a, other_b, (me % half).reshape(1), *gathered)
    received = mirrored(other_out)
    return pl.pallas_call(
        place_kernel,
        out_shape=jax.ShapeDtypeStruct((row_total, members * width), jnp.bfloat16),
        in_specs=[SMEM, VMEM, VMEM],
        out_specs=VMEM,
        compiler_params=SMALL,
        name="place",
    )((me // half).reshape(1), own_out, received)


def solution(mesh):
    return jax.shard_map(
        shards,
        mesh=mesh,
        in_specs=(
            P(("groups", "seq"), None),
            P(("groups", "seq"), None),
            P(("groups", "seq"), None),
            P(("groups", "seq"), None),
            P(("groups", "seq"), None),
            P(("groups", "seq"), None),
            P(None, "seq"),
        ),
        out_specs=P(("groups", "seq"), None),
        check_vma=False,
    )
```

```python
import functools
import math

import jax
import jax.numpy as jnp
from jax import lax
from jax.experimental import pallas as pl
from jax.experimental.pallas import tpu as pltpu
from jax.sharding import PartitionSpec as P


HQ = 16
KVH = 4
HD = 128
GROUP = HQ // KVH
LANES = 128
PARTS = 4
STAT_ROWS = KVH * PARTS
SCALE2 = math.log2(math.e) / math.sqrt(HD)
CHUNK = 512
FLOOR = -(2.0**100)


def iota(shape, axis):
    return lax.broadcasted_iota(jnp.int32, shape, axis)


def fill_slots(page_list, base, members, capacity, source, count):
    tiles, width = page_list.shape

    def clear(i, carry):
        source[i] = -1
        return carry

    lax.fori_loop(0, members * capacity, clear, 0)

    def clear_count(i, carry):
        count[i] = 0
        return carry

    lax.fori_loop(0, members, clear_count, 0)
    for tile in range(tiles):
        for item in range(width):
            page = page_list[tile, item] - base

            @pl.when((page >= 0) & (page < members))
            def _():
                slot = count[page]
                source[page * capacity + slot] = tile
                count[page] = slot + 1


def pack_kernel(members, capacity, base, page_list, queries, packed, source, count):
    tiles = page_list.shape[0]
    rows = queries.shape[0]
    tile_rows = rows // tiles
    slot_rows = capacity * tile_rows
    block = GROUP * slot_rows
    fill_slots(page_list, base[0], members, capacity, source, count)
    row = iota((block, GROUP * rows), 0)
    col = iota((block, GROUP * rows), 1)
    fixed = (row // slot_rows == col // rows) & (row % tile_rows == col % tile_rows)
    slot = row % slot_rows // tile_rows
    tile = col % rows // tile_rows
    pieces = []
    for page in range(members):
        wanted = jnp.full((block, GROUP * rows), -1, jnp.int32)
        for k in range(capacity):
            wanted = jnp.where(slot == k, source[page * capacity + k], wanted)
        pieces.append((fixed & (tile == wanted)).astype(jnp.bfloat16))
    chosen = jnp.concatenate(pieces, axis=0)
    for group in range(KVH):
        stacked = jnp.concatenate(
            [
                queries[:, (group * GROUP + j) * HD : (group * GROUP + j + 1) * HD]
                for j in range(GROUP)
            ],
            axis=0,
        )
        sent = jnp.dot(chosen, stacked, preferred_element_type=jnp.float32).astype(jnp.bfloat16)
        packed[:, group * block : (group + 1) * block, :] = sent.reshape(members, block, HD)


def attend_kernel(queries, keys, values, partial, stats):
    members, block, _ = queries.shape
    rows = members * block
    group = pl.program_id(0)
    asked = queries[...].reshape(rows, HD)
    page = keys.shape[0]
    chunk = min(CHUNK, page)
    ones = jnp.ones((chunk, HD), jnp.bfloat16)
    highest = None
    total = None
    for start in range(0, page, chunk):
        scores = lax.dot_general(
            asked,
            keys[start : start + chunk, :],
            (((1,), (1,)), ((), ())),
            preferred_element_type=jnp.float32,
        )
        here = jnp.max(scores, axis=1, keepdims=True)
        new = here if highest is None else jnp.maximum(highest, here)
        weights = jnp.exp2((scores - new) * SCALE2).astype(jnp.bfloat16)
        extended = jnp.concatenate([values[start : start + chunk, :], ones], axis=1)
        mixed = jnp.dot(weights, extended, preferred_element_type=jnp.float32)
        if total is None:
            total = mixed
        else:
            total = total * jnp.exp2((highest - new) * SCALE2) + mixed
        highest = new
    summed = total[:, HD:]
    result = (total[:, :HD] / summed).astype(jnp.bfloat16).reshape(members, block, HD)
    partial[:, pl.ds(pl.multiple_of(group * block, block), block), :] = result
    peak = jnp.broadcast_to(highest * SCALE2, (rows, LANES))
    peak_high = peak.astype(jnp.bfloat16).astype(jnp.float32)
    peak_low = (peak - peak_high).astype(jnp.bfloat16).astype(jnp.float32)
    moved = summed * jnp.exp2(peak - peak_high - peak_low)
    moved_high = moved.astype(jnp.bfloat16).astype(jnp.float32)
    moved_low = moved - moved_high
    part = iota((rows, LANES), 1) % PARTS
    mixed = jnp.where(
        part == 0,
        peak_high,
        jnp.where(part == 1, peak_low, jnp.where(part == 2, moved_high, moved_low)),
    )
    turned = mixed.T[:STAT_ROWS, :]
    mine = iota((STAT_ROWS, rows), 0) // PARTS == group

    @pl.when(group == 0)
    def _():
        stats[...] = turned

    @pl.when(group > 0)
    def _():
        stats[...] = jnp.where(mine, turned, stats[...])

    @pl.when(group == KVH - 1)
    def _():
        padded = jnp.concatenate(
            [stats[...], jnp.zeros((STAT_ROWS, LANES), jnp.float32)], axis=1
        )
        for member in range(members):
            partial[member, KVH * block :, :] = padded[
                :, member * block : member * block + LANES
            ].astype(jnp.bfloat16)


def split(value):
    high = value.astype(jnp.bfloat16).astype(jnp.float32)
    return high, (value - high).astype(jnp.bfloat16).astype(jnp.float32)


def stacked_heads(queries, group):
    return jnp.concatenate(
        [
            queries[:, (group * GROUP + j) * HD : (group * GROUP + j + 1) * HD]
            for j in range(GROUP)
        ],
        axis=0,
    )


def own_partial(queries, new_keys, new_values, causal, group):
    scores = lax.dot_general(
        stacked_heads(queries, group),
        new_keys[:, group * HD : (group + 1) * HD],
        (((1,), (1,)), ((), ())),
        preferred_element_type=jnp.float32,
    )
    scores = jnp.where(causal, scores, -jnp.inf)
    peak = jnp.max(scores, axis=1, keepdims=True)
    weights = jnp.exp2((scores - peak) * SCALE2)
    total = jnp.sum(weights, axis=1, keepdims=True)
    mixed = jnp.dot(
        weights.astype(jnp.bfloat16),
        new_values[:, group * HD : (group + 1) * HD],
        preferred_element_type=jnp.float32,
    )
    return peak * SCALE2, total, mixed


def merge_kernel(members, capacity, with_own, base, page_list, *refs):
    own_refs = refs[:3] if with_own else ()
    returned, merged, source, count = refs[len(own_refs) :]
    tiles = page_list.shape[0]
    tall = (merged.shape[0] - STAT_ROWS) // KVH
    rows = tall // GROUP
    tile_rows = rows // tiles
    slot_rows = capacity * tile_rows
    block = GROUP * slot_rows
    width = members * block
    fill_slots(page_list, base[0], members, capacity, source, count)
    lane = iota((8, width), 1)
    lane_slot = lane // block * capacity + lane % slot_rows // tile_rows
    wanted = jnp.full((8, width), -1, jnp.int32)
    for slot in range(members * capacity):
        wanted = jnp.where(lane_slot == slot, source[slot], wanted)
    lane_code = (wanted * tile_rows + lane % tile_rows) + (lane % block // slot_rows) * rows
    lane_code = jnp.where(wanted < 0, -1, lane_code)[:1, :]
    bias = jnp.where(iota((tall, width), 0) == lane_code, 0.0, -jnp.inf)
    stat_pieces = [
        returned[member, KVH * block :, :].astype(jnp.float32)[:, :block]
        for member in range(members)
    ]
    stats = jnp.concatenate(stat_pieces, axis=1)
    if with_own:
        own_row = iota((tall, rows), 0) % rows
        own_col = iota((tall, rows), 1)
        causal = (own_row // tile_rows == own_col // tile_rows) & (own_col <= own_row)
    part = iota((tall, LANES), 1)
    columns = jnp.zeros((tall, LANES), jnp.float32)
    for group in range(KVH):
        at = group * PARTS
        peak = bias + (stats[at : at + 1, :] + stats[at + 1 : at + 2, :])
        moved = stats[at + 2 : at + 3, :] + stats[at + 3 : at + 4, :]
        top = jnp.maximum(jnp.max(peak, axis=1, keepdims=True), FLOOR)
        if with_own:
            own_peak, own_total, own_sum = own_partial(*own_refs, causal, group)
            top = jnp.maximum(top, own_peak)
        factor = jnp.exp2(peak - top) * moved
        denom = jnp.sum(factor, axis=1, keepdims=True)
        if with_own:
            own_factor = jnp.exp2(own_peak - top)
            denom = denom + own_factor * own_total
        inverse = 1.0 / jnp.where(denom > 0.0, denom, 1.0)
        factor = factor * inverse
        high = factor.astype(jnp.bfloat16)
        low = (factor - high.astype(jnp.float32)).astype(jnp.bfloat16)
        outs = returned[:, group * block : (group + 1) * block, :].reshape(width, HD)
        numer = jnp.dot(high, outs, preferred_element_type=jnp.float32) + jnp.dot(
            low, outs, preferred_element_type=jnp.float32
        )
        if with_own:
            numer = numer + own_factor * inverse * own_sum
        merged[group * tall : (group + 1) * tall, :] = numer.astype(jnp.bfloat16)
        peak_high, peak_low = split(top)
        moved_high, moved_low = split(denom * jnp.exp2(top - peak_high - peak_low))
        for i, value in enumerate((peak_high, peak_low, moved_high, moved_low)):
            columns = jnp.where(part == at + i, value, columns)
    merged[KVH * tall :, :tall] = columns.T[:STAT_ROWS, :].astype(jnp.bfloat16)


def combine(tall, first, second):
    rows = tall // GROUP
    a = first[KVH * tall :, :].astype(jnp.float32)
    b = second[KVH * tall :, :].astype(jnp.float32)
    shares = []
    for group in range(KVH):
        at = group * PARTS
        a_peak = a[at : at + 1, :] + a[at + 1 : at + 2, :]
        b_peak = b[at : at + 1, :] + b[at + 1 : at + 2, :]
        a_total = a[at + 2 : at + 3, :] + a[at + 3 : at + 4, :]
        b_total = b[at + 2 : at + 3, :] + b[at + 3 : at + 4, :]
        top = jnp.maximum(a_peak, b_peak)
        a_factor = a_total * jnp.exp2(a_peak - top)
        b_factor = b_total * jnp.exp2(b_peak - top)
        denom = a_factor + b_factor
        shares += [a_factor / denom, b_factor / denom]
    shares = jnp.concatenate(
        shares + [jnp.zeros((LANES - len(shares), LANES), jnp.float32)], axis=0
    ).T
    heads = []
    for group in range(KVH):
        rows_at = slice(group * tall, (group + 1) * tall)
        mixed = (
            first[rows_at, :].astype(jnp.float32) * shares[:tall, 2 * group : 2 * group + 1]
            + second[rows_at, :].astype(jnp.float32)
            * shares[:tall, 2 * group + 1 : 2 * group + 2]
        ).astype(jnp.bfloat16)
        heads += [mixed[j * rows : (j + 1) * rows, :] for j in range(GROUP)]
    return jnp.concatenate(heads, axis=1)


def attended_kernel(first, second, attended):
    tall = (first.shape[0] - STAT_ROWS) // KVH
    attended[...] = combine(tall, first, second)


def project_kernel(count, places, own_a, own_b, other_a, other_b, me, *refs):
    weights = refs[: len(places)]
    own_out, other_out = refs[len(places) :]
    width = weights[0].shape[1]
    tall = (own_a.shape[0] - STAT_ROWS) // KVH
    rows = tall // GROUP
    left = jnp.concatenate(
        [combine(tall, own_a, own_b), combine(tall, other_a, other_b)], axis=0
    )
    for k in range(count):
        made = sum(
            jnp.dot(
                left[:, start : start + weights[i].shape[0]],
                weights[i][...],
                preferred_element_type=jnp.float32,
            )
            for i, (shard, start) in enumerate(places)
            if shard == k
        ).astype(jnp.bfloat16)
        at = pl.ds(pl.multiple_of((me[0] ^ k) * width, width), width)
        own_out[:, at] = made[:rows, :]
        other_out[:, at] = made[rows:, :]


def place_kernel(first, own, received, out):
    width = own.shape[1]
    out[:, pl.ds(pl.multiple_of(first[0] * width, width), width)] = own[...]
    out[:, pl.ds(pl.multiple_of((1 - first[0]) * width, width), width)] = received[...]


VMEM = pl.BlockSpec(memory_space=pltpu.VMEM)
SMEM = pl.BlockSpec(memory_space=pltpu.SMEM)
PROJECT = pltpu.CompilerParams(vmem_limit_bytes=16 << 20)
LARGE = pltpu.CompilerParams(vmem_limit_bytes=60 << 20)
SMALL = pltpu.CompilerParams(vmem_limit_bytes=16 << 20)


def slot_scratch(members, capacity):
    return [
        pltpu.SMEM((members * capacity,), jnp.int32),
        pltpu.SMEM((members,), jnp.int32),
    ]


def on_chip(array):
    return pltpu.with_memory_space_constraint(array, pltpu.VMEM)


def in_hbm(array):
    return pltpu.with_memory_space_constraint(array, pltpu.HBM)


def early_first(step):
    return (1, 0) if step == 2 else (0, 1)


def shards(queries, new_keys, new_values, keys, values, page_list, out_weight):
    members = lax.axis_size("seq")
    me = lax.axis_index("seq")
    tile_count, list_width = page_list.shape
    row_total, features = queries.shape
    tile_rows = row_total // tile_count
    capacity = max(1, 2 * tile_count * list_width // members)
    block = GROUP * capacity * tile_rows
    half = members // 2
    tall = GROUP * row_total
    halves = [list(range(half)), list(range(half, members))]
    base = (me // half * half).reshape(1)
    page = keys.shape[0]
    rows = half * block

    def mirrored(array):
        return lax.ppermute(array, "seq", [(i, (i + half) % members) for i in range(members)])

    def pack(tiles, listed, params):
        return pl.pallas_call(
            functools.partial(pack_kernel, half, capacity),
            out_shape=jax.ShapeDtypeStruct((half, KVH * block, HD), jnp.bfloat16),
            in_specs=[SMEM, SMEM, VMEM],
            out_specs=VMEM,
            scratch_shapes=slot_scratch(half, capacity),
            compiler_params=params,
            name="pack",
        )(base, listed, tiles)

    def spread(array):
        return lax.all_to_all(
            array, "seq", split_axis=0, concat_axis=0, tiled=True, axis_index_groups=halves
        )

    def attend(incoming):
        return pl.pallas_call(
            attend_kernel,
            out_shape=jax.ShapeDtypeStruct((half, KVH * block + STAT_ROWS, HD), jnp.bfloat16),
            grid=(KVH,),
            in_specs=[
                pl.BlockSpec((half, block, HD), lambda g: (0, g, 0)),
                pl.BlockSpec((page, HD), lambda g: (0, g)),
                pl.BlockSpec((page, HD), lambda g: (0, g)),
            ],
            out_specs=pl.BlockSpec((half, KVH * block + STAT_ROWS, HD), lambda g: (0, 0, 0)),
            scratch_shapes=[pltpu.VMEM((STAT_ROWS, rows), jnp.float32)],
            compiler_params=pltpu.CompilerParams(
                dimension_semantics=("arbitrary",), vmem_limit_bytes=24 << 20
            ),
            cost_estimate=pl.CostEstimate(
                flops=4 * rows * KVH * page * HD,
                bytes_accessed=4 * page * KVH * HD,
                transcendentals=rows * KVH * page,
            ),
            name="attend",
        )(incoming, in_hbm(keys), in_hbm(values))

    def merge(listed, returned, own):
        return pl.pallas_call(
            functools.partial(merge_kernel, half, capacity, bool(own)),
            out_shape=jax.ShapeDtypeStruct((KVH * tall + STAT_ROWS, HD), jnp.bfloat16),
            in_specs=[SMEM, SMEM] + [VMEM] * (len(own) + 1),
            out_specs=VMEM,
            scratch_shapes=slot_scratch(half, capacity),
            compiler_params=SMALL,
            name="merge",
        )(base, listed, *own, returned)

    other_queries = mirrored(queries)
    other_list = mirrored(page_list)
    packed_near = pack(queries, page_list, LARGE)
    near = spread(packed_near)
    packed_far = pack(other_queries, other_list, SMALL)
    far = spread(packed_far)
    near_partial = attend(near)
    near_back = spread(near_partial)
    far_partial = attend(far)
    far_back = spread(far_partial)
    own_a = merge(page_list, near_back, (queries, new_keys, new_values))
    other_b = merge(other_list, far_back, ())
    other_a = mirrored(own_a)
    own_b = mirrored(other_b)

    width = out_weight.shape[1]
    if width % LANES or members & (members - 1):
        attended = pl.pallas_call(
            attended_kernel,
            out_shape=jax.ShapeDtypeStruct((row_total, features), jnp.bfloat16),
            in_specs=[VMEM, VMEM],
            out_specs=VMEM,
            name="combine",
        )(own_a, own_b)
        return jnp.dot(
            attended,
            lax.all_gather(out_weight, "seq", axis=1, tiled=True),
            preferred_element_type=jnp.float32,
        ).astype(jnp.bfloat16)

    def exchanged(array, step):
        return lax.ppermute(array, "seq", [(i, i ^ step) for i in range(members)])

    middle = features // 2
    halves_of = [out_weight[:middle, :], out_weight[middle:, :]]
    pieces = {0: [out_weight]}
    for step in range(2, half, 2):
        low = step & -step
        if low == step:
            pieces[step] = [None, None]
            for i in early_first(step):
                pieces[step][i] = exchanged(halves_of[i], step)
    for step in range(2, half, 2):
        low = step & -step
        if low != step:
            first_piece = exchanged(pieces[step ^ low][0], low)
            pieces[step] = [first_piece, exchanged(pieces[low][1], step ^ low)]
    gathered = []
    places = []
    for step, parts in pieces.items():
        for i, part in enumerate(parts):
            gathered += [part, exchanged(part, 1)]
            places += [(step, i * middle), (step + 1, i * middle)]
    own_out, other_out = pl.pallas_call(
        functools.partial(project_kernel, half, tuple(places)),
        out_shape=[jax.ShapeDtypeStruct((row_total, half * width), jnp.bfloat16)] * 2,
        in_specs=[VMEM] * 4 + [SMEM] + [VMEM] * len(places),
        out_specs=[VMEM, VMEM],
        compiler_params=PROJECT,
        name="project",
    )(own_a, own_b, other_a, other_b, (me % half).reshape(1), *[on_chip(part) for part in gathered])
    received = mirrored(other_out)
    return pl.pallas_call(
        place_kernel,
        out_shape=jax.ShapeDtypeStruct((row_total, members * width), jnp.bfloat16),
        in_specs=[SMEM, VMEM, VMEM],
        out_specs=VMEM,
        compiler_params=SMALL,
        name="place",
    )((me // half).reshape(1), own_out, received)


def solution(mesh):
    return jax.shard_map(
        shards,
        mesh=mesh,
        in_specs=(
            P(("groups", "seq"), None),
            P(("groups", "seq"), None),
            P(("groups", "seq"), None),
            P(("groups", "seq"), None),
            P(("groups", "seq"), None),
            P(("groups", "seq"), None),
            P(None, "seq"),
        ),
        out_specs=P(("groups", "seq"), None),
        check_vma=False,
    )
```

```python
import functools
import math

import jax
import jax.numpy as jnp
from jax import lax
from jax.experimental import pallas as pl
from jax.experimental.pallas import tpu as pltpu
from jax.sharding import PartitionSpec as P


HQ = 16
KVH = 4
HD = 128
GROUP = HQ // KVH
LANES = 128
PARTS = 4
STAT_ROWS = KVH * PARTS
SCALE2 = math.log2(math.e) / math.sqrt(HD)
CHUNK = 512
FLOOR = -(2.0**100)


def iota(shape, axis):
    return lax.broadcasted_iota(jnp.int32, shape, axis)


def slot_codes(listed, base, members, capacity, tile):
    width, tiles = listed.shape
    entry = [[listed[k : k + 1, t : t + 1] for t in range(tiles)] for k in range(width)]
    codes = []
    for k in range(width):
        page = jnp.zeros_like(tile)
        for t in range(tiles):
            page = jnp.where(tile == t, entry[k][t], page)
        slot = jnp.zeros_like(tile)
        for t in range(tiles):
            earlier = tile > t
            for other in range(width):
                slot = slot + jnp.where(earlier & (page == entry[other][t]), 1, 0)
        page = page - base
        inside = (page >= 0) & (page < members)
        codes.append(jnp.where(inside, page * capacity + slot, -1))
    return codes


def pack_kernel(members, capacity, base, listed, queries, packed):
    tiles = listed.shape[1]
    rows = queries.shape[0]
    tile_rows = rows // tiles
    slot_rows = capacity * tile_rows
    block = GROUP * slot_rows
    tall = GROUP * rows
    codes = slot_codes(
        listed, base[0], members, capacity, iota((8, tall), 1) % rows // tile_rows
    )
    row = iota((block, tall), 0)
    col = iota((block, tall), 1)
    fixed = (row // slot_rows == col // rows) & (row % tile_rows == col % tile_rows)
    slot = jnp.where(fixed, row % slot_rows // tile_rows, -2 - members * capacity)
    pieces = []
    for page in range(members):
        here = slot + page * capacity
        hit = codes[0][:1, :] == here
        for code in codes[1:]:
            hit = hit | (code[:1, :] == here)
        pieces.append(jnp.where(hit, 1.0, 0.0).astype(jnp.bfloat16))
    chosen = jnp.concatenate(pieces, axis=0)
    for group in range(KVH):
        sent = jnp.dot(
            chosen, stacked_heads(queries, group), preferred_element_type=jnp.float32
        ).astype(jnp.bfloat16)
        packed[:, group * block : (group + 1) * block, :] = sent.reshape(members, block, HD)


def attend_kernel(queries, keys, values, partial, stats):
    members, block, _ = queries.shape
    rows = members * block
    group = pl.program_id(0)
    asked = queries[...].reshape(rows, HD)
    page = keys.shape[0]
    chunk = min(CHUNK, page)
    ones = jnp.ones((chunk, HD), jnp.bfloat16)
    highest = None
    total = None
    for start in range(0, page, chunk):
        scores = lax.dot_general(
            asked,
            keys[start : start + chunk, :],
            (((1,), (1,)), ((), ())),
            preferred_element_type=jnp.float32,
        )
        here = jnp.max(scores, axis=1, keepdims=True)
        new = here if highest is None else jnp.maximum(highest, here)
        weights = jnp.exp2((scores - new) * SCALE2).astype(jnp.bfloat16)
        extended = jnp.concatenate([values[start : start + chunk, :], ones], axis=1)
        mixed = jnp.dot(weights, extended, preferred_element_type=jnp.float32)
        if total is None:
            total = mixed
        else:
            total = total * jnp.exp2((highest - new) * SCALE2) + mixed
        highest = new
    summed = total[:, HD:]
    result = (total[:, :HD] / summed).astype(jnp.bfloat16).reshape(members, block, HD)
    partial[:, pl.ds(pl.multiple_of(group * block, block), block), :] = result
    peak = jnp.broadcast_to(highest * SCALE2, (rows, LANES))
    peak_high = peak.astype(jnp.bfloat16).astype(jnp.float32)
    peak_low = (peak - peak_high).astype(jnp.bfloat16).astype(jnp.float32)
    moved = summed * jnp.exp2(peak - peak_high - peak_low)
    moved_high = moved.astype(jnp.bfloat16).astype(jnp.float32)
    moved_low = moved - moved_high
    part = iota((rows, LANES), 1) % PARTS
    mixed = jnp.where(
        part == 0,
        peak_high,
        jnp.where(part == 1, peak_low, jnp.where(part == 2, moved_high, moved_low)),
    )
    turned = mixed.T[:STAT_ROWS, :]
    mine = iota((STAT_ROWS, rows), 0) // PARTS == group

    @pl.when(group == 0)
    def _():
        stats[...] = turned

    @pl.when(group > 0)
    def _():
        stats[...] = jnp.where(mine, turned, stats[...])

    @pl.when(group == KVH - 1)
    def _():
        padded = jnp.concatenate(
            [stats[...], jnp.zeros((STAT_ROWS, LANES), jnp.float32)], axis=1
        )
        for member in range(members):
            partial[member, KVH * block :, :] = padded[
                :, member * block : member * block + LANES
            ].astype(jnp.bfloat16)


def split(value):
    high = value.astype(jnp.bfloat16).astype(jnp.float32)
    return high, (value - high).astype(jnp.bfloat16).astype(jnp.float32)


def stacked_heads(queries, group):
    return jnp.concatenate(
        [
            queries[:, (group * GROUP + j) * HD : (group * GROUP + j + 1) * HD]
            for j in range(GROUP)
        ],
        axis=0,
    )


def own_partial(queries, new_keys, new_values, causal, group):
    scores = lax.dot_general(
        stacked_heads(queries, group),
        new_keys[:, group * HD : (group + 1) * HD],
        (((1,), (1,)), ((), ())),
        preferred_element_type=jnp.float32,
    )
    scores = jnp.where(causal, scores, -jnp.inf)
    peak = jnp.max(scores, axis=1, keepdims=True)
    weights = jnp.exp2((scores - peak) * SCALE2)
    total = jnp.sum(weights, axis=1, keepdims=True)
    mixed = jnp.dot(
        weights.astype(jnp.bfloat16),
        new_values[:, group * HD : (group + 1) * HD],
        preferred_element_type=jnp.float32,
    )
    return peak * SCALE2, total, mixed


def merge_kernel(members, capacity, with_own, base, listed, *refs):
    own_refs = refs[:3] if with_own else ()
    returned, merged = refs[len(own_refs) :]
    tiles = listed.shape[1]
    tall = (merged.shape[0] - STAT_ROWS) // KVH
    rows = tall // GROUP
    tile_rows = rows // tiles
    slot_rows = capacity * tile_rows
    block = GROUP * slot_rows
    width = members * block
    across = iota((8, tall), 1)
    codes = slot_codes(listed, base[0], members, capacity, across % rows // tile_rows)
    turned = jnp.full((8, tall), -1, jnp.int32)
    for k, code in enumerate(codes):
        code = (code * GROUP + across // rows) * tile_rows + across % tile_rows
        turned = jnp.where(iota((8, tall), 0) == k, code, turned)
    turned = jnp.concatenate(
        [turned.astype(jnp.float32), jnp.zeros((LANES - 8, tall), jnp.float32)], axis=0
    ).T.astype(jnp.int32)
    lane = iota((8, width), 1)
    lane_code = lane // block * capacity + lane % slot_rows // tile_rows
    lane_code = (lane_code * GROUP + lane % block // slot_rows) * tile_rows + lane % tile_rows
    hit = turned[:, :1] == lane_code[:1, :]
    for k in range(1, len(codes)):
        hit = hit | (turned[:, k : k + 1] == lane_code[:1, :])
    bias = jnp.where(hit, 0.0, -jnp.inf)
    stat_pieces = [
        returned[member, KVH * block :, :].astype(jnp.float32)[:, :block]
        for member in range(members)
    ]
    stats = jnp.concatenate(stat_pieces, axis=1)
    if with_own:
        own_row = iota((tall, rows), 0) % rows
        own_col = iota((tall, rows), 1)
        causal = (own_row // tile_rows == own_col // tile_rows) & (own_col <= own_row)
    part = iota((tall, LANES), 1)
    columns = jnp.zeros((tall, LANES), jnp.float32)
    for group in range(KVH):
        at = group * PARTS
        peak = bias + (stats[at : at + 1, :] + stats[at + 1 : at + 2, :])
        moved = stats[at + 2 : at + 3, :] + stats[at + 3 : at + 4, :]
        top = jnp.maximum(jnp.max(peak, axis=1, keepdims=True), FLOOR)
        if with_own:
            own_peak, own_total, own_sum = own_partial(*own_refs, causal, group)
            top = jnp.maximum(top, own_peak)
        factor = jnp.exp2(peak - top) * moved
        denom = jnp.sum(factor, axis=1, keepdims=True)
        if with_own:
            own_factor = jnp.exp2(own_peak - top)
            denom = denom + own_factor * own_total
        inverse = 1.0 / jnp.where(denom > 0.0, denom, 1.0)
        factor = factor * inverse
        high = factor.astype(jnp.bfloat16)
        low = (factor - high.astype(jnp.float32)).astype(jnp.bfloat16)
        outs = returned[:, group * block : (group + 1) * block, :].reshape(width, HD)
        numer = jnp.dot(high, outs, preferred_element_type=jnp.float32) + jnp.dot(
            low, outs, preferred_element_type=jnp.float32
        )
        if with_own:
            numer = numer + own_factor * inverse * own_sum
        merged[group * tall : (group + 1) * tall, :] = numer.astype(jnp.bfloat16)
        peak_high, peak_low = split(top)
        moved_high, moved_low = split(denom * jnp.exp2(top - peak_high - peak_low))
        for i, value in enumerate((peak_high, peak_low, moved_high, moved_low)):
            columns = jnp.where(part == at + i, value, columns)
    merged[KVH * tall :, :tall] = columns.T[:STAT_ROWS, :].astype(jnp.bfloat16)


def combine(tall, first, second):
    rows = tall // GROUP
    a = first[KVH * tall :, :].astype(jnp.float32)
    b = second[KVH * tall :, :].astype(jnp.float32)
    shares = []
    for group in range(KVH):
        at = group * PARTS
        a_peak = a[at : at + 1, :] + a[at + 1 : at + 2, :]
        b_peak = b[at : at + 1, :] + b[at + 1 : at + 2, :]
        a_total = a[at + 2 : at + 3, :] + a[at + 3 : at + 4, :]
        b_total = b[at + 2 : at + 3, :] + b[at + 3 : at + 4, :]
        top = jnp.maximum(a_peak, b_peak)
        a_factor = a_total * jnp.exp2(a_peak - top)
        b_factor = b_total * jnp.exp2(b_peak - top)
        denom = a_factor + b_factor
        shares += [a_factor / denom, b_factor / denom]
    shares = jnp.concatenate(
        shares + [jnp.zeros((LANES - len(shares), LANES), jnp.float32)], axis=0
    ).T
    heads = []
    for group in range(KVH):
        rows_at = slice(group * tall, (group + 1) * tall)
        mixed = (
            first[rows_at, :].astype(jnp.float32) * shares[:tall, 2 * group : 2 * group + 1]
            + second[rows_at, :].astype(jnp.float32)
            * shares[:tall, 2 * group + 1 : 2 * group + 2]
        ).astype(jnp.bfloat16)
        heads += [mixed[j * rows : (j + 1) * rows, :] for j in range(GROUP)]
    return jnp.concatenate(heads, axis=1)


def attended_kernel(first, second, attended):
    tall = (first.shape[0] - STAT_ROWS) // KVH
    attended[...] = combine(tall, first, second)


def project_kernel(count, places, own_a, own_b, other_a, other_b, me, *refs):
    weights = refs[: len(places)]
    own_out, other_out = refs[len(places) :]
    width = weights[0].shape[1]
    tall = (own_a.shape[0] - STAT_ROWS) // KVH
    rows = tall // GROUP
    left = jnp.concatenate(
        [combine(tall, own_a, own_b), combine(tall, other_a, other_b)], axis=0
    )
    for k in range(count):
        made = sum(
            jnp.dot(
                left[:, start : start + weights[i].shape[0]],
                weights[i][...],
                preferred_element_type=jnp.float32,
            )
            for i, (shard, start) in enumerate(places)
            if shard == k
        ).astype(jnp.bfloat16)
        at = pl.ds(pl.multiple_of((me[0] ^ k) * width, width), width)
        own_out[:, at] = made[:rows, :]
        other_out[:, at] = made[rows:, :]


def place_kernel(first, own, received, out):
    width = own.shape[1]
    out[:, pl.ds(pl.multiple_of(first[0] * width, width), width)] = own[...]
    out[:, pl.ds(pl.multiple_of((1 - first[0]) * width, width), width)] = received[...]


VMEM = pl.BlockSpec(memory_space=pltpu.VMEM)
SMEM = pl.BlockSpec(memory_space=pltpu.SMEM)
PROJECT = pltpu.CompilerParams(vmem_limit_bytes=16 << 20)
LARGE = pltpu.CompilerParams(vmem_limit_bytes=60 << 20)
SMALL = pltpu.CompilerParams(vmem_limit_bytes=16 << 20)


def on_chip(array):
    return pltpu.with_memory_space_constraint(array, pltpu.VMEM)


def in_hbm(array):
    return pltpu.with_memory_space_constraint(array, pltpu.HBM)


def early_first(step):
    return (1, 0) if step == 2 else (0, 1)


def shards(queries, new_keys, new_values, keys, values, page_list, out_weight):
    members = lax.axis_size("seq")
    me = lax.axis_index("seq")
    tile_count, list_width = page_list.shape
    row_total, features = queries.shape
    tile_rows = row_total // tile_count
    capacity = max(1, 2 * tile_count * list_width // members)
    block = GROUP * capacity * tile_rows
    half = members // 2
    tall = GROUP * row_total
    halves = [list(range(half)), list(range(half, members))]
    base = (me // half * half).reshape(1)
    page = keys.shape[0]
    rows = half * block

    def mirrored(array):
        return lax.ppermute(array, "seq", [(i, (i + half) % members) for i in range(members)])

    def pack(tiles, listed, params):
        return pl.pallas_call(
            functools.partial(pack_kernel, half, capacity),
            out_shape=jax.ShapeDtypeStruct((half, KVH * block, HD), jnp.bfloat16),
            in_specs=[SMEM, VMEM, VMEM],
            out_specs=VMEM,
            compiler_params=params,
            name="pack",
        )(base, listed, tiles)

    def spread(array):
        return lax.all_to_all(
            array, "seq", split_axis=0, concat_axis=0, tiled=True, axis_index_groups=halves
        )

    def attend(incoming):
        return pl.pallas_call(
            attend_kernel,
            out_shape=jax.ShapeDtypeStruct((half, KVH * block + STAT_ROWS, HD), jnp.bfloat16),
            grid=(KVH,),
            in_specs=[
                pl.BlockSpec((half, block, HD), lambda g: (0, g, 0)),
                pl.BlockSpec((page, HD), lambda g: (0, g)),
                pl.BlockSpec((page, HD), lambda g: (0, g)),
            ],
            out_specs=pl.BlockSpec((half, KVH * block + STAT_ROWS, HD), lambda g: (0, 0, 0)),
            scratch_shapes=[pltpu.VMEM((STAT_ROWS, rows), jnp.float32)],
            compiler_params=pltpu.CompilerParams(
                dimension_semantics=("arbitrary",), vmem_limit_bytes=24 << 20
            ),
            cost_estimate=pl.CostEstimate(
                flops=4 * rows * KVH * page * HD,
                bytes_accessed=4 * page * KVH * HD,
                transcendentals=rows * KVH * page,
            ),
            name="attend",
        )(incoming, in_hbm(keys), in_hbm(values))

    def merge(listed, returned, own):
        return pl.pallas_call(
            functools.partial(merge_kernel, half, capacity, bool(own)),
            out_shape=jax.ShapeDtypeStruct((KVH * tall + STAT_ROWS, HD), jnp.bfloat16),
            in_specs=[SMEM] + [VMEM] * (len(own) + 2),
            out_specs=VMEM,
            compiler_params=SMALL,
            name="merge",
        )(base, listed, *own, returned)

    own_list = page_list.T
    other_queries = mirrored(queries)
    other_list = mirrored(own_list)
    packed_near = pack(queries, own_list, LARGE)
    near = spread(packed_near)
    packed_far = pack(other_queries, other_list, SMALL)
    far = spread(packed_far)
    near_partial = attend(near)
    near_back = spread(near_partial)
    far_partial = attend(far)
    far_back = spread(far_partial)
    own_a = merge(own_list, near_back, (queries, new_keys, new_values))
    other_b = merge(other_list, far_back, ())
    other_a = mirrored(own_a)
    own_b = mirrored(other_b)

    width = out_weight.shape[1]
    if width % LANES or members & (members - 1):
        attended = pl.pallas_call(
            attended_kernel,
            out_shape=jax.ShapeDtypeStruct((row_total, features), jnp.bfloat16),
            in_specs=[VMEM, VMEM],
            out_specs=VMEM,
            name="combine",
        )(own_a, own_b)
        return jnp.dot(
            attended,
            lax.all_gather(out_weight, "seq", axis=1, tiled=True),
            preferred_element_type=jnp.float32,
        ).astype(jnp.bfloat16)

    def exchanged(array, step):
        return lax.ppermute(array, "seq", [(i, i ^ step) for i in range(members)])

    middle = features // 2
    halves_of = [out_weight[:middle, :], out_weight[middle:, :]]
    pieces = {0: [out_weight]}
    for step in range(2, half, 2):
        low = step & -step
        if low == step:
            pieces[step] = [None, None]
            for i in early_first(step):
                pieces[step][i] = exchanged(halves_of[i], step)
    for step in range(2, half, 2):
        low = step & -step
        if low != step:
            first_piece = exchanged(pieces[step ^ low][0], low)
            pieces[step] = [first_piece, exchanged(pieces[low][1], step ^ low)]
    gathered = []
    places = []
    for step, parts in pieces.items():
        for i, part in enumerate(parts):
            gathered += [part, exchanged(part, 1)]
            places += [(step, i * middle), (step + 1, i * middle)]
    own_out, other_out = pl.pallas_call(
        functools.partial(project_kernel, half, tuple(places)),
        out_shape=[jax.ShapeDtypeStruct((row_total, half * width), jnp.bfloat16)] * 2,
        in_specs=[VMEM] * 4 + [SMEM] + [VMEM] * len(places),
        out_specs=[VMEM, VMEM],
        compiler_params=PROJECT,
        name="project",
    )(own_a, own_b, other_a, other_b, (me % half).reshape(1), *[on_chip(part) for part in gathered])
    received = mirrored(other_out)
    return pl.pallas_call(
        place_kernel,
        out_shape=jax.ShapeDtypeStruct((row_total, members * width), jnp.bfloat16),
        in_specs=[SMEM, VMEM, VMEM],
        out_specs=VMEM,
        compiler_params=SMALL,
        name="place",
    )((me // half).reshape(1), own_out, received)


def solution(mesh):
    return jax.shard_map(
        shards,
        mesh=mesh,
        in_specs=(
            P(("groups", "seq"), None),
            P(("groups", "seq"), None),
            P(("groups", "seq"), None),
            P(("groups", "seq"), None),
            P(("groups", "seq"), None),
            P(("groups", "seq"), None),
            P(None, "seq"),
        ),
        out_specs=P(("groups", "seq"), None),
        check_vma=False,
    )
```

```python
import functools
import math

import jax
import jax.numpy as jnp
from jax import lax
from jax.experimental import pallas as pl
from jax.experimental.pallas import tpu as pltpu
from jax.sharding import PartitionSpec as P


HQ = 16
KVH = 4
HD = 128
GROUP = HQ // KVH
LANES = 128
PARTS = 4
STAT_ROWS = KVH * PARTS
SCALE2 = math.log2(math.e) / math.sqrt(HD)
CHUNK = 512
FLOOR = -(2.0**100)


def iota(shape, axis):
    return lax.broadcasted_iota(jnp.int32, shape, axis)


def slot_codes(listed, base, members, capacity, tile):
    width, tiles = listed.shape
    entry = [[listed[k : k + 1, t : t + 1] for t in range(tiles)] for k in range(width)]
    codes = []
    for k in range(width):
        page = jnp.zeros_like(tile)
        for t in range(tiles):
            page = jnp.where(tile == t, entry[k][t], page)
        slot = jnp.zeros_like(tile)
        for t in range(tiles):
            earlier = tile > t
            for other in range(width):
                slot = slot + jnp.where(earlier & (page == entry[other][t]), 1, 0)
        page = page - base
        inside = (page >= 0) & (page < members)
        codes.append(jnp.where(inside, page * capacity + slot, -1))
    return codes


def pack_kernel(members, capacity, base, listed, queries, packed):
    tiles = listed.shape[1]
    rows = queries.shape[0]
    tile_rows = rows // tiles
    slot_rows = capacity * tile_rows
    block = GROUP * slot_rows
    tall = GROUP * rows
    codes = slot_codes(
        listed, base[0], members, capacity, iota((8, tall), 1) % rows // tile_rows
    )
    row = iota((block, tall), 0)
    col = iota((block, tall), 1)
    fixed = (row // slot_rows == col // rows) & (row % tile_rows == col % tile_rows)
    slot = jnp.where(fixed, row % slot_rows // tile_rows, -2 - members * capacity)
    pieces = []
    for page in range(members):
        here = slot + page * capacity
        hit = codes[0][:1, :] == here
        for code in codes[1:]:
            hit = hit | (code[:1, :] == here)
        pieces.append(jnp.where(hit, 1.0, 0.0).astype(jnp.bfloat16))
    chosen = jnp.concatenate(pieces, axis=0)
    for group in range(KVH):
        sent = jnp.dot(
            chosen, stacked_heads(queries, group), preferred_element_type=jnp.float32
        ).astype(jnp.bfloat16)
        packed[:, group * block : (group + 1) * block, :] = sent.reshape(members, block, HD)


def attend_kernel(queries, keys, values, partial, stats):
    members, block, _ = queries.shape
    rows = members * block
    group = pl.program_id(0)
    asked = queries[...].reshape(rows, HD)
    page = keys.shape[0]
    chunk = min(CHUNK, page)
    ones = jnp.ones((chunk, HD), jnp.bfloat16)
    highest = None
    total = None
    for start in range(0, page, chunk):
        scores = lax.dot_general(
            asked,
            keys[start : start + chunk, :],
            (((1,), (1,)), ((), ())),
            preferred_element_type=jnp.float32,
        )
        here = jnp.max(scores, axis=1, keepdims=True)
        new = here if highest is None else jnp.maximum(highest, here)
        weights = jnp.exp2((scores - new) * SCALE2).astype(jnp.bfloat16)
        extended = jnp.concatenate([values[start : start + chunk, :], ones], axis=1)
        mixed = jnp.dot(weights, extended, preferred_element_type=jnp.float32)
        if total is None:
            total = mixed
        else:
            total = total * jnp.exp2((highest - new) * SCALE2) + mixed
        highest = new
    summed = total[:, HD:]
    result = (total[:, :HD] / summed).astype(jnp.bfloat16).reshape(members, block, HD)
    partial[:, pl.ds(pl.multiple_of(group * block, block), block), :] = result
    peak = jnp.broadcast_to(highest * SCALE2, (rows, LANES))
    peak_high = peak.astype(jnp.bfloat16).astype(jnp.float32)
    peak_low = (peak - peak_high).astype(jnp.bfloat16).astype(jnp.float32)
    moved = summed * jnp.exp2(peak - peak_high - peak_low)
    moved_high = moved.astype(jnp.bfloat16).astype(jnp.float32)
    moved_low = moved - moved_high
    part = iota((rows, LANES), 1) % PARTS
    mixed = jnp.where(
        part == 0,
        peak_high,
        jnp.where(part == 1, peak_low, jnp.where(part == 2, moved_high, moved_low)),
    )
    turned = mixed.T[:STAT_ROWS, :]
    mine = iota((STAT_ROWS, rows), 0) // PARTS == group

    @pl.when(group == 0)
    def _():
        stats[...] = turned

    @pl.when(group > 0)
    def _():
        stats[...] = jnp.where(mine, turned, stats[...])

    @pl.when(group == KVH - 1)
    def _():
        padded = jnp.concatenate(
            [stats[...], jnp.zeros((STAT_ROWS, LANES), jnp.float32)], axis=1
        )
        for member in range(members):
            partial[member, KVH * block :, :] = padded[
                :, member * block : member * block + LANES
            ].astype(jnp.bfloat16)


def split(value):
    high = value.astype(jnp.bfloat16).astype(jnp.float32)
    return high, (value - high).astype(jnp.bfloat16).astype(jnp.float32)


def stacked_heads(queries, group):
    return jnp.concatenate(
        [
            queries[:, (group * GROUP + j) * HD : (group * GROUP + j + 1) * HD]
            for j in range(GROUP)
        ],
        axis=0,
    )


def own_partial(queries, new_keys, new_values, causal, group):
    scores = lax.dot_general(
        stacked_heads(queries, group),
        new_keys[:, group * HD : (group + 1) * HD],
        (((1,), (1,)), ((), ())),
        preferred_element_type=jnp.float32,
    )
    scores = jnp.where(causal, scores, -jnp.inf)
    peak = jnp.max(scores, axis=1, keepdims=True)
    weights = jnp.exp2((scores - peak) * SCALE2)
    total = jnp.sum(weights, axis=1, keepdims=True)
    mixed = jnp.dot(
        weights.astype(jnp.bfloat16),
        new_values[:, group * HD : (group + 1) * HD],
        preferred_element_type=jnp.float32,
    )
    return peak * SCALE2, total, mixed


def merge_kernel(members, capacity, with_own, base, listed, *refs):
    own_refs = refs[:3] if with_own else ()
    returned, merged = refs[len(own_refs) :]
    tiles = listed.shape[1]
    tall = (merged.shape[0] - STAT_ROWS) // KVH
    rows = tall // GROUP
    tile_rows = rows // tiles
    slot_rows = capacity * tile_rows
    block = GROUP * slot_rows
    width = members * block
    across = iota((8, tall), 1)
    codes = slot_codes(listed, base[0], members, capacity, across % rows // tile_rows)
    turned = jnp.full((8, tall), -1, jnp.int32)
    for k, code in enumerate(codes):
        code = (code * GROUP + across // rows) * tile_rows + across % tile_rows
        turned = jnp.where(iota((8, tall), 0) == k, code, turned)
    turned = jnp.concatenate(
        [turned.astype(jnp.float32), jnp.zeros((LANES - 8, tall), jnp.float32)], axis=0
    ).T.astype(jnp.int32)
    lane = iota((8, width), 1)
    lane_code = lane // block * capacity + lane % slot_rows // tile_rows
    lane_code = (lane_code * GROUP + lane % block // slot_rows) * tile_rows + lane % tile_rows
    hit = turned[:, :1] == lane_code[:1, :]
    for k in range(1, len(codes)):
        hit = hit | (turned[:, k : k + 1] == lane_code[:1, :])
    bias = jnp.where(hit, 0.0, -jnp.inf)
    stat_pieces = [
        returned[member, KVH * block :, :].astype(jnp.float32)[:, :block]
        for member in range(members)
    ]
    stats = jnp.concatenate(stat_pieces, axis=1)
    if with_own:
        own_row = iota((tall, rows), 0) % rows
        own_col = iota((tall, rows), 1)
        causal = (own_row // tile_rows == own_col // tile_rows) & (own_col <= own_row)
    part = iota((tall, LANES), 1)
    columns = jnp.zeros((tall, LANES), jnp.float32)
    for group in range(KVH):
        at = group * PARTS
        peak = bias + (stats[at : at + 1, :] + stats[at + 1 : at + 2, :])
        moved = stats[at + 2 : at + 3, :] + stats[at + 3 : at + 4, :]
        top = jnp.maximum(jnp.max(peak, axis=1, keepdims=True), FLOOR)
        if with_own:
            own_peak, own_total, own_sum = own_partial(*own_refs, causal, group)
            top = jnp.maximum(top, own_peak)
        factor = jnp.exp2(peak - top) * moved
        denom = jnp.sum(factor, axis=1, keepdims=True)
        if with_own:
            own_factor = jnp.exp2(own_peak - top)
            denom = denom + own_factor * own_total
        inverse = 1.0 / jnp.where(denom > 0.0, denom, 1.0)
        factor = factor * inverse
        high = factor.astype(jnp.bfloat16)
        low = (factor - high.astype(jnp.float32)).astype(jnp.bfloat16)
        outs = returned[:, group * block : (group + 1) * block, :].reshape(width, HD)
        numer = jnp.dot(high, outs, preferred_element_type=jnp.float32) + jnp.dot(
            low, outs, preferred_element_type=jnp.float32
        )
        if with_own:
            numer = numer + own_factor * inverse * own_sum
        merged[group * tall : (group + 1) * tall, :] = numer.astype(jnp.bfloat16)
        peak_high, peak_low = split(top)
        moved_high, moved_low = split(denom * jnp.exp2(top - peak_high - peak_low))
        for i, value in enumerate((peak_high, peak_low, moved_high, moved_low)):
            columns = jnp.where(part == at + i, value, columns)
    merged[KVH * tall :, :tall] = columns.T[:STAT_ROWS, :].astype(jnp.bfloat16)


def combine(tall, first, second):
    rows = tall // GROUP
    a = first[KVH * tall :, :].astype(jnp.float32)
    b = second[KVH * tall :, :].astype(jnp.float32)
    shares = []
    for group in range(KVH):
        at = group * PARTS
        a_peak = a[at : at + 1, :] + a[at + 1 : at + 2, :]
        b_peak = b[at : at + 1, :] + b[at + 1 : at + 2, :]
        a_total = a[at + 2 : at + 3, :] + a[at + 3 : at + 4, :]
        b_total = b[at + 2 : at + 3, :] + b[at + 3 : at + 4, :]
        top = jnp.maximum(a_peak, b_peak)
        a_factor = a_total * jnp.exp2(a_peak - top)
        b_factor = b_total * jnp.exp2(b_peak - top)
        denom = a_factor + b_factor
        shares += [a_factor / denom, b_factor / denom]
    shares = jnp.concatenate(
        shares + [jnp.zeros((LANES - len(shares), LANES), jnp.float32)], axis=0
    ).T
    heads = []
    for group in range(KVH):
        rows_at = slice(group * tall, (group + 1) * tall)
        mixed = (
            first[rows_at, :].astype(jnp.float32) * shares[:tall, 2 * group : 2 * group + 1]
            + second[rows_at, :].astype(jnp.float32)
            * shares[:tall, 2 * group + 1 : 2 * group + 2]
        ).astype(jnp.bfloat16)
        heads += [mixed[j * rows : (j + 1) * rows, :] for j in range(GROUP)]
    return jnp.concatenate(heads, axis=1)


def attended_kernel(first, second, attended):
    tall = (first.shape[0] - STAT_ROWS) // KVH
    attended[...] = combine(tall, first, second)


def project_kernel(own_a, own_b, other_a, other_b, places, *refs):
    weights = refs[:-2]
    own_out, other_out = refs[-2:]
    width = weights[0].shape[1]
    tall = (own_a.shape[0] - STAT_ROWS) // KVH
    rows = tall // GROUP
    left = jnp.concatenate(
        [combine(tall, own_a, own_b), combine(tall, other_a, other_b)], axis=0
    )
    for i, weight in enumerate(weights):
        made = jnp.dot(left, weight[...], preferred_element_type=jnp.float32)
        made = made.astype(jnp.bfloat16)
        at = pl.ds(pl.multiple_of(places[i] * width, width), width)
        own_out[:, at] = made[:rows, :]
        other_out[:, at] = made[rows:, :]


def place_kernel(first, own, received, out):
    width = own.shape[1]
    out[:, pl.ds(pl.multiple_of(first[0] * width, width), width)] = own[...]
    out[:, pl.ds(pl.multiple_of((1 - first[0]) * width, width), width)] = received[...]


VMEM = pl.BlockSpec(memory_space=pltpu.VMEM)
SMEM = pl.BlockSpec(memory_space=pltpu.SMEM)
PROJECT = pltpu.CompilerParams(vmem_limit_bytes=16 << 20)
LARGE = pltpu.CompilerParams(vmem_limit_bytes=60 << 20)
SMALL = pltpu.CompilerParams(vmem_limit_bytes=16 << 20)


def on_chip(array):
    return pltpu.with_memory_space_constraint(array, pltpu.VMEM)


def in_hbm(array):
    return pltpu.with_memory_space_constraint(array, pltpu.HBM)


def shards(queries, new_keys, new_values, keys, values, page_list, out_weight):
    members = lax.axis_size("seq")
    me = lax.axis_index("seq")
    tile_count, list_width = page_list.shape
    row_total, features = queries.shape
    tile_rows = row_total // tile_count
    capacity = max(1, 2 * tile_count * list_width // members)
    block = GROUP * capacity * tile_rows
    half = members // 2
    tall = GROUP * row_total
    halves = [list(range(half)), list(range(half, members))]
    base = (me // half * half).reshape(1)
    page = keys.shape[0]
    rows = half * block

    def mirrored(array):
        return lax.ppermute(array, "seq", [(i, (i + half) % members) for i in range(members)])

    def pack(tiles, listed, params):
        return pl.pallas_call(
            functools.partial(pack_kernel, half, capacity),
            out_shape=jax.ShapeDtypeStruct((half, KVH * block, HD), jnp.bfloat16),
            in_specs=[SMEM, VMEM, VMEM],
            out_specs=VMEM,
            compiler_params=params,
            name="pack",
        )(base, listed, tiles)

    def spread(array):
        return lax.all_to_all(
            array, "seq", split_axis=0, concat_axis=0, tiled=True, axis_index_groups=halves
        )

    def attend(incoming):
        return pl.pallas_call(
            attend_kernel,
            out_shape=jax.ShapeDtypeStruct((half, KVH * block + STAT_ROWS, HD), jnp.bfloat16),
            grid=(KVH,),
            in_specs=[
                pl.BlockSpec((half, block, HD), lambda g: (0, g, 0)),
                pl.BlockSpec((page, HD), lambda g: (0, g)),
                pl.BlockSpec((page, HD), lambda g: (0, g)),
            ],
            out_specs=pl.BlockSpec((half, KVH * block + STAT_ROWS, HD), lambda g: (0, 0, 0)),
            scratch_shapes=[pltpu.VMEM((STAT_ROWS, rows), jnp.float32)],
            compiler_params=pltpu.CompilerParams(
                dimension_semantics=("arbitrary",), vmem_limit_bytes=24 << 20
            ),
            cost_estimate=pl.CostEstimate(
                flops=4 * rows * KVH * page * HD,
                bytes_accessed=4 * page * KVH * HD,
                transcendentals=rows * KVH * page,
            ),
            name="attend",
        )(incoming, in_hbm(keys), in_hbm(values))

    def merge(listed, returned, own):
        return pl.pallas_call(
            functools.partial(merge_kernel, half, capacity, bool(own)),
            out_shape=jax.ShapeDtypeStruct((KVH * tall + STAT_ROWS, HD), jnp.bfloat16),
            in_specs=[SMEM] + [VMEM] * (len(own) + 2),
            out_specs=VMEM,
            compiler_params=SMALL,
            name="merge",
        )(base, listed, *own, returned)

    own_list = page_list.T
    other_queries = mirrored(queries)
    other_list = mirrored(own_list)
    packed_near = pack(queries, own_list, LARGE)
    near = spread(packed_near)
    packed_far = pack(other_queries, other_list, SMALL)
    far = spread(packed_far)
    near_partial = attend(near)
    near_back = spread(near_partial)
    far_partial = attend(far)
    far_back = spread(far_partial)
    own_a = merge(own_list, near_back, (queries, new_keys, new_values))
    other_b = merge(other_list, far_back, ())
    other_a = mirrored(own_a)
    own_b = mirrored(other_b)

    width = out_weight.shape[1]
    if width % LANES or members & (members - 1):
        attended = pl.pallas_call(
            attended_kernel,
            out_shape=jax.ShapeDtypeStruct((row_total, features), jnp.bfloat16),
            in_specs=[VMEM, VMEM],
            out_specs=VMEM,
            name="combine",
        )(own_a, own_b)
        return jnp.dot(
            attended,
            lax.all_gather(out_weight, "seq", axis=1, tiled=True),
            preferred_element_type=jnp.float32,
        ).astype(jnp.bfloat16)

    def exchanged(array, even_step, odd_step):
        return lax.ppermute(
            array,
            "seq",
            [(i, i ^ (odd_step if i & 1 else even_step)) for i in range(members)],
        )

    steps = [(0, 0)]
    arrays = [out_weight]
    if half == 8:
        arrays.append(exchanged(out_weight, 2, 4))
        arrays.append(exchanged(out_weight, 4, 2))
        arrays.append(exchanged(arrays[1], 4, 2))
        steps += [(2, 4), (4, 2), (6, 6)]
    else:
        for step in range(2, half, 2):
            arrays.append(exchanged(out_weight, step, step))
            steps.append((step, step))
    gathered = []
    places = []
    for array, (even, odd) in zip(arrays, steps):
        gathered += [array, exchanged(array, 1, 1)]
        places += [(even, odd), (odd ^ 1, even ^ 1)]
    odd_core = me % 2
    places = jnp.stack(
        [(me % half) ^ (even + odd_core * (odd - even)) for even, odd in places]
    ).astype(jnp.int32)
    own_out, other_out = pl.pallas_call(
        project_kernel,
        out_shape=[jax.ShapeDtypeStruct((row_total, half * width), jnp.bfloat16)] * 2,
        in_specs=[VMEM] * 4 + [SMEM] + [VMEM] * half,
        out_specs=[VMEM, VMEM],
        compiler_params=PROJECT,
        name="project",
    )(own_a, own_b, other_a, other_b, places, *[on_chip(part) for part in gathered])
    received = mirrored(other_out)
    return pl.pallas_call(
        place_kernel,
        out_shape=jax.ShapeDtypeStruct((row_total, members * width), jnp.bfloat16),
        in_specs=[SMEM, VMEM, VMEM],
        out_specs=VMEM,
        compiler_params=SMALL,
        name="place",
    )((me // half).reshape(1), own_out, received)


def solution(mesh):
    return jax.shard_map(
        shards,
        mesh=mesh,
        in_specs=(
            P(("groups", "seq"), None),
            P(("groups", "seq"), None),
            P(("groups", "seq"), None),
            P(("groups", "seq"), None),
            P(("groups", "seq"), None),
            P(("groups", "seq"), None),
            P(None, "seq"),
        ),
        out_specs=P(("groups", "seq"), None),
        check_vma=False,
    )
```

```python
import functools
import math

import jax
import jax.numpy as jnp
from jax import lax
from jax.experimental import pallas as pl
from jax.experimental.pallas import tpu as pltpu
from jax.sharding import PartitionSpec as P


HQ = 16
KVH = 4
HD = 128
GROUP = HQ // KVH
LANES = 128
PARTS = 4
STAT_ROWS = KVH * PARTS
SCALE2 = math.log2(math.e) / math.sqrt(HD)
CHUNK = 512
FLOOR = -(2.0**100)


def iota(shape, axis):
    return lax.broadcasted_iota(jnp.int32, shape, axis)


def slot_codes(listed, base, members, capacity, tile):
    width, tiles = listed.shape
    entry = [[listed[k : k + 1, t : t + 1] for t in range(tiles)] for k in range(width)]
    codes = []
    for k in range(width):
        page = jnp.zeros_like(tile)
        for t in range(tiles):
            page = jnp.where(tile == t, entry[k][t], page)
        slot = jnp.zeros_like(tile)
        for t in range(tiles):
            earlier = tile > t
            for other in range(width):
                slot = slot + jnp.where(earlier & (page == entry[other][t]), 1, 0)
        page = page - base
        inside = (page >= 0) & (page < members)
        codes.append(jnp.where(inside, page * capacity + slot, -1))
    return codes


def pack_kernel(members, capacity, base, listed, queries, packed):
    tiles = listed.shape[1]
    rows = queries.shape[0]
    tile_rows = rows // tiles
    slot_rows = capacity * tile_rows
    block = GROUP * slot_rows
    tall = GROUP * rows
    codes = slot_codes(
        listed, base[0], members, capacity, iota((8, tall), 1) % rows // tile_rows
    )
    row = iota((block, tall), 0)
    col = iota((block, tall), 1)
    fixed = (row // slot_rows == col // rows) & (row % tile_rows == col % tile_rows)
    slot = jnp.where(fixed, row % slot_rows // tile_rows, -2 - members * capacity)
    pieces = []
    for page in range(members):
        here = slot + page * capacity
        hit = codes[0][:1, :] == here
        for code in codes[1:]:
            hit = hit | (code[:1, :] == here)
        pieces.append(jnp.where(hit, 1.0, 0.0).astype(jnp.bfloat16))
    chosen = jnp.concatenate(pieces, axis=0)
    for group in range(KVH):
        sent = jnp.dot(
            chosen, stacked_heads(queries, group), preferred_element_type=jnp.float32
        ).astype(jnp.bfloat16)
        packed[:, group * block : (group + 1) * block, :] = sent.reshape(members, block, HD)


def attend_kernel(queries, keys, values, partial, stats):
    members, block, _ = queries.shape
    rows = members * block
    group = pl.program_id(0)
    asked = queries[...].reshape(rows, HD)
    page = keys.shape[0]
    chunk = min(CHUNK, page)
    ones = jnp.ones((chunk, HD), jnp.bfloat16)
    highest = None
    total = None
    for start in range(0, page, chunk):
        scores = lax.dot_general(
            asked,
            keys[start : start + chunk, :],
            (((1,), (1,)), ((), ())),
            preferred_element_type=jnp.float32,
        )
        here = jnp.max(scores, axis=1, keepdims=True)
        new = here if highest is None else jnp.maximum(highest, here)
        weights = jnp.exp2((scores - new) * SCALE2).astype(jnp.bfloat16)
        extended = jnp.concatenate([values[start : start + chunk, :], ones], axis=1)
        mixed = jnp.dot(weights, extended, preferred_element_type=jnp.float32)
        if total is None:
            total = mixed
        else:
            total = total * jnp.exp2((highest - new) * SCALE2) + mixed
        highest = new
    summed = total[:, HD:]
    result = (total[:, :HD] / summed).astype(jnp.bfloat16).reshape(members, block, HD)
    partial[:, pl.ds(pl.multiple_of(group * block, block), block), :] = result
    peak = jnp.broadcast_to(highest * SCALE2, (rows, LANES))
    peak_high = peak.astype(jnp.bfloat16).astype(jnp.float32)
    peak_low = (peak - peak_high).astype(jnp.bfloat16).astype(jnp.float32)
    moved = summed * jnp.exp2(peak - peak_high - peak_low)
    moved_high = moved.astype(jnp.bfloat16).astype(jnp.float32)
    moved_low = moved - moved_high
    part = iota((rows, LANES), 1) % PARTS
    mixed = jnp.where(
        part == 0,
        peak_high,
        jnp.where(part == 1, peak_low, jnp.where(part == 2, moved_high, moved_low)),
    )
    turned = mixed.T[:STAT_ROWS, :]
    mine = iota((STAT_ROWS, rows), 0) // PARTS == group

    @pl.when(group == 0)
    def _():
        stats[...] = turned

    @pl.when(group > 0)
    def _():
        stats[...] = jnp.where(mine, turned, stats[...])

    @pl.when(group == KVH - 1)
    def _():
        padded = jnp.concatenate(
            [stats[...], jnp.zeros((STAT_ROWS, LANES), jnp.float32)], axis=1
        )
        for member in range(members):
            partial[member, KVH * block :, :] = padded[
                :, member * block : member * block + LANES
            ].astype(jnp.bfloat16)


def split(value):
    high = value.astype(jnp.bfloat16).astype(jnp.float32)
    return high, (value - high).astype(jnp.bfloat16).astype(jnp.float32)


def stacked_heads(queries, group):
    return jnp.concatenate(
        [
            queries[:, (group * GROUP + j) * HD : (group * GROUP + j + 1) * HD]
            for j in range(GROUP)
        ],
        axis=0,
    )


def own_partial(queries, new_keys, new_values, causal, group):
    scores = lax.dot_general(
        stacked_heads(queries, group),
        new_keys[:, group * HD : (group + 1) * HD],
        (((1,), (1,)), ((), ())),
        preferred_element_type=jnp.float32,
    )
    scores = jnp.where(causal, scores, -jnp.inf)
    peak = jnp.max(scores, axis=1, keepdims=True)
    weights = jnp.exp2((scores - peak) * SCALE2)
    total = jnp.sum(weights, axis=1, keepdims=True)
    mixed = jnp.dot(
        weights.astype(jnp.bfloat16),
        new_values[:, group * HD : (group + 1) * HD],
        preferred_element_type=jnp.float32,
    )
    return peak * SCALE2, total, mixed


def merge_kernel(members, capacity, with_own, base, listed, *refs):
    own_refs = refs[:3] if with_own else ()
    returned, merged = refs[len(own_refs) :]
    tiles = listed.shape[1]
    tall = (merged.shape[0] - STAT_ROWS) // KVH
    rows = tall // GROUP
    tile_rows = rows // tiles
    slot_rows = capacity * tile_rows
    block = GROUP * slot_rows
    width = members * block
    across = iota((8, tall), 1)
    codes = slot_codes(listed, base[0], members, capacity, across % rows // tile_rows)
    turned = jnp.full((8, tall), -1, jnp.int32)
    for k, code in enumerate(codes):
        code = (code * GROUP + across // rows) * tile_rows + across % tile_rows
        turned = jnp.where(iota((8, tall), 0) == k, code, turned)
    turned = jnp.concatenate(
        [turned.astype(jnp.float32), jnp.zeros((LANES - 8, tall), jnp.float32)], axis=0
    ).T.astype(jnp.int32)
    lane = iota((8, width), 1)
    lane_code = lane // block * capacity + lane % slot_rows // tile_rows
    lane_code = (lane_code * GROUP + lane % block // slot_rows) * tile_rows + lane % tile_rows
    hit = turned[:, :1] == lane_code[:1, :]
    for k in range(1, len(codes)):
        hit = hit | (turned[:, k : k + 1] == lane_code[:1, :])
    bias = jnp.where(hit, 0.0, -jnp.inf)
    stat_pieces = [
        returned[member, KVH * block :, :].astype(jnp.float32)[:, :block]
        for member in range(members)
    ]
    stats = jnp.concatenate(stat_pieces, axis=1)
    if with_own:
        own_row = iota((tall, rows), 0) % rows
        own_col = iota((tall, rows), 1)
        causal = (own_row // tile_rows == own_col // tile_rows) & (own_col <= own_row)
    part = iota((tall, LANES), 1)
    columns = jnp.zeros((tall, LANES), jnp.float32)
    for group in range(KVH):
        at = group * PARTS
        peak = bias + (stats[at : at + 1, :] + stats[at + 1 : at + 2, :])
        moved = stats[at + 2 : at + 3, :] + stats[at + 3 : at + 4, :]
        top = jnp.maximum(jnp.max(peak, axis=1, keepdims=True), FLOOR)
        if with_own:
            own_peak, own_total, own_sum = own_partial(*own_refs, causal, group)
            top = jnp.maximum(top, own_peak)
        factor = jnp.exp2(peak - top) * moved
        denom = jnp.sum(factor, axis=1, keepdims=True)
        if with_own:
            own_factor = jnp.exp2(own_peak - top)
            denom = denom + own_factor * own_total
        inverse = 1.0 / jnp.where(denom > 0.0, denom, 1.0)
        factor = factor * inverse
        high = factor.astype(jnp.bfloat16)
        low = (factor - high.astype(jnp.float32)).astype(jnp.bfloat16)
        outs = returned[:, group * block : (group + 1) * block, :].reshape(width, HD)
        numer = jnp.dot(high, outs, preferred_element_type=jnp.float32) + jnp.dot(
            low, outs, preferred_element_type=jnp.float32
        )
        if with_own:
            numer = numer + own_factor * inverse * own_sum
        merged[group * tall : (group + 1) * tall, :] = numer.astype(jnp.bfloat16)
        peak_high, peak_low = split(top)
        moved_high, moved_low = split(denom * jnp.exp2(top - peak_high - peak_low))
        for i, value in enumerate((peak_high, peak_low, moved_high, moved_low)):
            columns = jnp.where(part == at + i, value, columns)
    merged[KVH * tall :, :tall] = columns.T[:STAT_ROWS, :].astype(jnp.bfloat16)


def combine(tall, first, second):
    rows = tall // GROUP
    a = first[KVH * tall :, :].astype(jnp.float32)
    b = second[KVH * tall :, :].astype(jnp.float32)
    shares = []
    for group in range(KVH):
        at = group * PARTS
        a_peak = a[at : at + 1, :] + a[at + 1 : at + 2, :]
        b_peak = b[at : at + 1, :] + b[at + 1 : at + 2, :]
        a_total = a[at + 2 : at + 3, :] + a[at + 3 : at + 4, :]
        b_total = b[at + 2 : at + 3, :] + b[at + 3 : at + 4, :]
        top = jnp.maximum(a_peak, b_peak)
        a_factor = a_total * jnp.exp2(a_peak - top)
        b_factor = b_total * jnp.exp2(b_peak - top)
        denom = a_factor + b_factor
        shares += [a_factor / denom, b_factor / denom]
    shares = jnp.concatenate(
        shares + [jnp.zeros((LANES - len(shares), LANES), jnp.float32)], axis=0
    ).T
    heads = []
    for group in range(KVH):
        rows_at = slice(group * tall, (group + 1) * tall)
        mixed = (
            first[rows_at, :].astype(jnp.float32) * shares[:tall, 2 * group : 2 * group + 1]
            + second[rows_at, :].astype(jnp.float32)
            * shares[:tall, 2 * group + 1 : 2 * group + 2]
        ).astype(jnp.bfloat16)
        heads += [mixed[j * rows : (j + 1) * rows, :] for j in range(GROUP)]
    return jnp.concatenate(heads, axis=1)


def attended_kernel(first, second, attended):
    tall = (first.shape[0] - STAT_ROWS) // KVH
    attended[...] = combine(tall, first, second)


def project_kernel(first, second, places, *refs):
    weights, out = refs[:-1], refs[-1]
    width = weights[0].shape[1]
    left = combine((first.shape[0] - STAT_ROWS) // KVH, first, second)
    for i, weight in enumerate(weights):
        made = jnp.dot(left, weight[...], preferred_element_type=jnp.float32)
        at = pl.ds(pl.multiple_of(places[i] * width, width), width)
        out[:, at] = made.astype(jnp.bfloat16)


def place_kernel(first, own, received, out):
    width = own.shape[1]
    out[:, pl.ds(pl.multiple_of(first[0] * width, width), width)] = own[...]
    out[:, pl.ds(pl.multiple_of((1 - first[0]) * width, width), width)] = received[...]


VMEM = pl.BlockSpec(memory_space=pltpu.VMEM)
SMEM = pl.BlockSpec(memory_space=pltpu.SMEM)
PROJECT = pltpu.CompilerParams(vmem_limit_bytes=16 << 20)
LARGE = pltpu.CompilerParams(vmem_limit_bytes=60 << 20)
SMALL = pltpu.CompilerParams(vmem_limit_bytes=16 << 20)


def on_chip(array):
    return pltpu.with_memory_space_constraint(array, pltpu.VMEM)


def in_hbm(array):
    return pltpu.with_memory_space_constraint(array, pltpu.HBM)


def shards(queries, new_keys, new_values, keys, values, page_list, out_weight):
    members = lax.axis_size("seq")
    me = lax.axis_index("seq")
    tile_count, list_width = page_list.shape
    row_total, features = queries.shape
    tile_rows = row_total // tile_count
    capacity = max(1, 2 * tile_count * list_width // members)
    block = GROUP * capacity * tile_rows
    half = members // 2
    tall = GROUP * row_total
    halves = [list(range(half)), list(range(half, members))]
    base = (me // half * half).reshape(1)
    page = keys.shape[0]
    rows = half * block

    def mirrored(array):
        return lax.ppermute(array, "seq", [(i, (i + half) % members) for i in range(members)])

    def pack(tiles, listed, params):
        return pl.pallas_call(
            functools.partial(pack_kernel, half, capacity),
            out_shape=jax.ShapeDtypeStruct((half, KVH * block, HD), jnp.bfloat16),
            in_specs=[SMEM, VMEM, VMEM],
            out_specs=VMEM,
            compiler_params=params,
            name="pack",
        )(base, listed, tiles)

    def spread(array):
        return lax.all_to_all(
            array, "seq", split_axis=0, concat_axis=0, tiled=True, axis_index_groups=halves
        )

    def attend(incoming):
        return pl.pallas_call(
            attend_kernel,
            out_shape=jax.ShapeDtypeStruct((half, KVH * block + STAT_ROWS, HD), jnp.bfloat16),
            grid=(KVH,),
            in_specs=[
                pl.BlockSpec((half, block, HD), lambda g: (0, g, 0)),
                pl.BlockSpec((page, HD), lambda g: (0, g)),
                pl.BlockSpec((page, HD), lambda g: (0, g)),
            ],
            out_specs=pl.BlockSpec((half, KVH * block + STAT_ROWS, HD), lambda g: (0, 0, 0)),
            scratch_shapes=[pltpu.VMEM((STAT_ROWS, rows), jnp.float32)],
            compiler_params=pltpu.CompilerParams(
                dimension_semantics=("arbitrary",), vmem_limit_bytes=24 << 20
            ),
            cost_estimate=pl.CostEstimate(
                flops=4 * rows * KVH * page * HD,
                bytes_accessed=4 * page * KVH * HD,
                transcendentals=rows * KVH * page,
            ),
            name="attend",
        )(incoming, in_hbm(keys), in_hbm(values))

    def merge(listed, returned, own):
        return pl.pallas_call(
            functools.partial(merge_kernel, half, capacity, bool(own)),
            out_shape=jax.ShapeDtypeStruct((KVH * tall + STAT_ROWS, HD), jnp.bfloat16),
            in_specs=[SMEM] + [VMEM] * (len(own) + 2),
            out_specs=VMEM,
            compiler_params=SMALL,
            name="merge",
        )(base, listed, *own, returned)

    own_list = page_list.T
    other_queries = mirrored(queries)
    other_list = mirrored(own_list)
    packed_near = pack(queries, own_list, LARGE)
    near = spread(packed_near)
    packed_far = pack(other_queries, other_list, SMALL)
    far = spread(packed_far)
    near_partial = attend(near)
    near_back = spread(near_partial)
    far_partial = attend(far)
    far_back = on_chip(spread(far_partial))
    own_a = merge(own_list, near_back, (queries, new_keys, new_values))
    other_b = merge(other_list, far_back, ())
    other_a = mirrored(own_a)
    own_b = mirrored(other_b)

    width = out_weight.shape[1]
    if width % LANES or members & (members - 1):
        attended = pl.pallas_call(
            attended_kernel,
            out_shape=jax.ShapeDtypeStruct((row_total, features), jnp.bfloat16),
            in_specs=[VMEM, VMEM],
            out_specs=VMEM,
            name="combine",
        )(own_a, own_b)
        return jnp.dot(
            attended,
            lax.all_gather(out_weight, "seq", axis=1, tiled=True),
            preferred_element_type=jnp.float32,
        ).astype(jnp.bfloat16)

    def exchanged(array, even_step, odd_step):
        return lax.ppermute(
            array,
            "seq",
            [(i, i ^ (odd_step if i & 1 else even_step)) for i in range(members)],
        )

    steps = [(0, 0)]
    arrays = [out_weight]
    if half == 8:
        arrays.append(exchanged(out_weight, 2, 4))
        arrays.append(exchanged(out_weight, 4, 2))
        arrays.append(exchanged(arrays[1], 4, 2))
        steps += [(2, 4), (4, 2), (6, 6)]
    else:
        for step in range(2, half, 2):
            arrays.append(exchanged(out_weight, step, step))
            steps.append((step, step))
    gathered = []
    places = []
    for array, (even, odd) in zip(arrays, steps):
        gathered += [array, exchanged(array, 1, 1)]
        places += [(even, odd), (odd ^ 1, even ^ 1)]
    odd_core = me % 2
    places = jnp.stack(
        [(me % half) ^ (even + odd_core * (odd - even)) for even, odd in places]
    ).astype(jnp.int32)
    gathered = [on_chip(part) for part in gathered]

    def project(first, second):
        return pl.pallas_call(
            project_kernel,
            out_shape=jax.ShapeDtypeStruct((row_total, half * width), jnp.bfloat16),
            in_specs=[VMEM] * 2 + [SMEM] + [VMEM] * half,
            out_specs=VMEM,
            compiler_params=PROJECT,
            name="project",
        )(first, second, places, *gathered)

    other_out = project(other_a, other_b)
    received = mirrored(other_out)
    own_out = project(own_a, own_b)
    return pl.pallas_call(
        place_kernel,
        out_shape=jax.ShapeDtypeStruct((row_total, members * width), jnp.bfloat16),
        in_specs=[SMEM, VMEM, VMEM],
        out_specs=VMEM,
        compiler_params=SMALL,
        name="place",
    )((me // half).reshape(1), own_out, received)


def solution(mesh):
    return jax.shard_map(
        shards,
        mesh=mesh,
        in_specs=(
            P(("groups", "seq"), None),
            P(("groups", "seq"), None),
            P(("groups", "seq"), None),
            P(("groups", "seq"), None),
            P(("groups", "seq"), None),
            P(("groups", "seq"), None),
            P(None, "seq"),
        ),
        out_specs=P(("groups", "seq"), None),
        check_vma=False,
    )
```
